256 devices in a mesh: dp: 4 (over x), tm: 8 (over z_hi, core), space: 8 (over y, z_lo).
Axes of the slice: x: 4, y: 4, z: 8 (z_hi: 4, z_lo: 2; z = z_hi * 2 + z_lo), core: 2. Of those that a mesh axis runs over, the one named last changes fastest.
Arguments:
- feats: bfloat16 [4, 8, 64, 128, 256], P('dp', 'tm', 'space'), may hold values from -6 to 6
- w_spatial: bfloat16 [3, 3, 256, 256], replicated, may hold values from -0.125 to 0.125
- w_temporal: bfloat16 [768, 256], replicated, may hold values from -0.21875 to 0.21875
- teacher_mid: bfloat16 [4, 8, 64, 128, 256], P('dp', 'tm', 'space'), may hold values from -6 to 6
- w_down: bfloat16 [2, 2, 256, 512], replicated, may hold values from -0.1875 to 0.1875
- w_query: bfloat16 [512, 512], replicated, may hold values from -8 to 8
- w_key: bfloat16 [512, 512], replicated, may hold values from -1 to 1
- w_value: bfloat16 [512, 512], replicated, may hold values from -0.25 to 0.25
- w_out: bfloat16 [512, 512], replicated, may hold values from -0.25 to 0.25
- teacher_top: bfloat16 [4, 8, 32, 64, 512], P('dp', 'tm', 'space'), may hold values from -6 to 6
Outputs:
- student_top: bfloat16 [4, 8, 32, 64, 512], P('dp', 'tm', 'space')
- grad_temporal: float32 [768, 256], P(('tm', 'space'))
- grad_out: float32 [512, 512], P(('tm', 'space'))
The draws below stay inside these ranges and needn't reach their ends.
All inputs are finite; a program needn't handle non-finite values.
Results may differ from the reference program's by a relative error of at most 0.0075.
Values may be sent and summed in bfloat16 or wider, within the bound.
No kernel may reach another device: no remote copies, remote signals or barrier semaphores. Data moves between devices by JAX's collectives and lax.ppermute only.
A program may use at most 64 MiB of HBM per device.

```python
import math
import jax
import jax.numpy as jnp
from jax import lax

C1 = 256
C2 = 512
KT = 3
W = 128
CLIPS = 4
FRAMES = 8
ROWS = 64


def paired_projections(key):
    base = jax.random.fold_in(key, 7)
    key_raw = jnp.clip(jax.random.normal(jax.random.fold_in(base, 1), (C2, C2), jnp.float32), -4.0, 4.0)
    query_raw = jnp.clip(jax.random.normal(jax.random.fold_in(base, 2), (C2, C2), jnp.float32), -4.0, 4.0)
    key_mat = key_raw / math.sqrt(C2)
    query_mat = query_raw / math.sqrt(C2)
    return (query_mat, key_mat)


def draw_w_query(key, part):
    return paired_projections(key)[0].astype(jnp.bfloat16)


def draw_w_key(key, part):
    return paired_projections(key)[1].astype(jnp.bfloat16)


def level_of(key, dims, pieces, smallest, high):
    def one(position, blocks):
        draws = jax.random.uniform(jax.random.fold_in(jax.random.fold_in(key, 6), position), (blocks,), jnp.float32, smallest / len(pieces), high / len(pieces))
        return jnp.repeat(jnp.exp(draws), dims[position] // blocks).reshape((-1,) + (1,) * (len(dims) - position - 1))

    level = one(*pieces[0])
    for cut in pieces[1:]:
        level = level * one(*cut)
    return level


def centred(stream_key, shape, deviation, limit, split=(), held_as=jnp.bfloat16):
    loudness = level_of(stream_key, shape, split, -0.22, 0.18) if split else 1.0
    drawn = jax.random.normal(stream_key, shape, jnp.float32) * deviation * loudness
    return jnp.minimum(jnp.maximum(drawn, -limit), limit).astype(held_as)


def setup_inputs(seed: int = 0) -> dict:
    seeds = jax.random.split(jax.random.key(seed), 11)
    feats = centred(seeds[0], (CLIPS, FRAMES, ROWS, W, C1), 1.0, 6.0, ((0, 4), (1, 8), (2, 8)))
    w_spatial = centred(seeds[1], (3, 3, C1, C1), (9 * C1) ** -0.5, 0.125)
    w_temporal = centred(seeds[2], (KT * C1, C1), (KT * C1) ** -0.5, 0.21875)
    teacher_mid = centred(seeds[3], (CLIPS, FRAMES, ROWS, W, C1), 1.0, 6.0, ((0, 4), (1, 8), (2, 8)))
    w_down = centred(seeds[4], (2, 2, C1, C2), (4 * C1) ** -0.5, 0.1875)
    w_query = draw_w_query(jax.random.fold_in(seeds[10], 71), 0)
    w_key = draw_w_key(jax.random.fold_in(seeds[10], 71), 0)
    w_value = centred(seeds[7], (C2, C2), C2 ** -0.5, 0.25)
    w_out = centred(seeds[8], (C2, C2), C2 ** -0.5, 0.25)
    teacher_top = centred(seeds[9], (CLIPS, FRAMES, ROWS // 2, W // 2, C2), 1.0, 6.0, ((0, 4), (1, 8), (2, 8)))
    return dict(feats=feats, w_spatial=w_spatial, w_temporal=w_temporal, teacher_mid=teacher_mid, w_down=w_down, w_query=w_query, w_key=w_key, w_value=w_value, w_out=w_out, teacher_top=teacher_top)


def reference(feats, w_spatial, w_temporal, teacher_mid, w_down, w_query, w_key, w_value, w_out, teacher_top):
    clips, frames, rows, cols, chan = feats.shape
    numbers = ('NHWC', 'HWIO', 'NHWC')
    flat = feats.reshape(clips * frames, rows, cols, chan)
    conv = lax.conv_general_dilated(flat, w_spatial, (1, 1), ((1, 1), (1, 1)), dimension_numbers=numbers, preferred_element_type=jnp.float32)
    spatial = jax.nn.silu(conv).astype(jnp.bfloat16).reshape(clips, frames, rows, cols, chan)
    zero = jnp.zeros_like(spatial[:, :1])
    back_one = jnp.concatenate([zero, spatial[:, :-1]], 1)[:, :frames]
    back_two = jnp.concatenate([zero, zero, spatial[:, :-2]], 1)[:, :frames]
    stacked = jnp.concatenate([back_two, back_one, spatial], -1).reshape(-1, 3 * chan)
    temporal = jnp.dot(stacked, w_temporal, preferred_element_type=jnp.float32)
    mid = (feats.reshape(-1, chan).astype(jnp.float32) + temporal).astype(jnp.bfloat16)
    diff_mid = (mid.astype(jnp.float32) - teacher_mid.reshape(-1, chan).astype(jnp.float32)).astype(jnp.bfloat16)
    scale_mid = 1.0 / math.sqrt(stacked.shape[0])
    grad_temporal = jnp.dot(stacked.T, diff_mid, preferred_element_type=jnp.float32) * scale_mid
    coarse = lax.conv_general_dilated(mid.reshape(clips * frames, rows, cols, chan), w_down, (2, 2), 'VALID', dimension_numbers=numbers, preferred_element_type=jnp.float32).astype(jnp.bfloat16)
    width = coarse.shape[-1]
    coarse = coarse.reshape(-1, width)
    query = jnp.dot(coarse, w_query, preferred_element_type=jnp.float32).astype(jnp.bfloat16)
    key = jnp.dot(coarse, w_key, preferred_element_type=jnp.float32).astype(jnp.bfloat16)
    value = jnp.dot(coarse, w_value, preferred_element_type=jnp.float32).astype(jnp.bfloat16)
    query = query.astype(jnp.float32).reshape(clips, frames, -1, width)
    key = key.astype(jnp.float32).reshape(clips, frames, -1, width)
    value = value.astype(jnp.float32).reshape(clips, frames, -1, width)
    scores = jnp.einsum('cqpd,ckpd->cpqk', query, key) * (1.0 / math.sqrt(width))
    later = jnp.arange(frames)[:, None] >= jnp.arange(frames)[None, :]
    scores = jnp.where(later[None, None], scores, -jnp.inf)
    top_score = lax.optimization_barrier(jnp.max(scores, -1, keepdims=True))
    weights = jnp.exp(scores - top_score)
    totals = lax.optimization_barrier(jnp.sum(weights, -1))
    attended = jnp.einsum('cpqk,ckpd->cqpd', weights, value) / jnp.transpose(totals, (0, 2, 1))[..., None]
    attended = attended.astype(jnp.bfloat16).reshape(-1, width)
    out = jnp.dot(attended, w_out, preferred_element_type=jnp.float32)
    student = (coarse.astype(jnp.float32) + out).astype(jnp.bfloat16)
    diff_top = (student.astype(jnp.float32) - teacher_top.reshape(-1, width).astype(jnp.float32)).astype(jnp.bfloat16)
    scale_top = 1.0 / math.sqrt(attended.shape[0])
    grad_out = jnp.dot(attended.T, diff_top, preferred_element_type=jnp.float32) * scale_top
    return (student.reshape(teacher_top.shape), grad_temporal, grad_out)
```

```python
import math

import jax
import jax.numpy as jnp
from jax import lax
from jax.sharding import PartitionSpec as P

F32 = jnp.float32
BF16 = jnp.bfloat16


def reduce_shares(grad):
    frames = lax.axis_size("tm")
    spaces = lax.axis_size("space")
    clips = lax.axis_size("dp")
    rows, cols = grad.shape
    piece = rows // (frames * spaces)
    halves = grad.reshape(frames // 2, 2, spaces, piece, cols)
    core = lax.axis_index("tm") % 2
    keep = lax.dynamic_index_in_dim(halves, core, 1, keepdims=False)
    give = lax.dynamic_index_in_dim(halves, 1 - core, 1, keepdims=False)
    got = lax.ppermute(give, "tm", [(i, i ^ 1) for i in range(frames)])
    part = (keep + got).transpose(1, 0, 2, 3).astype(BF16)
    part = lax.all_to_all(part, "space", 0, 0, tiled=True)
    part = jnp.sum(part.astype(F32), 0).astype(BF16)
    groups = [list(range(c, frames, 2)) for c in range(2)]
    part = lax.all_to_all(part, "tm", 0, 0, axis_index_groups=groups, tiled=True)
    part = jnp.sum(part.astype(F32), 0)
    others = [
        lax.ppermute(part, "dp", [(i, (i + k) % clips) for i in range(clips)])
        for k in range(1, clips)
    ]
    for other in others:
        part = part + other
    return part


def local(
    feats, w_spatial, w_temporal, teacher_mid, w_down, w_query, w_key, w_value, w_out, teacher_top
):
    numbers = ("NHWC", "HWIO", "NHWC")
    frames = lax.axis_size("tm")
    spaces = lax.axis_size("space")
    devices_all = lax.axis_size("dp") * frames * spaces
    frame_in = feats[0, 0]
    rows, cols, chan = frame_in.shape
    strip = cols // frames

    wide = jnp.pad(frame_in, ((0, 0), (1, 1), (0, 0)))
    windows = jnp.stack([wide[:, j * strip : j * strip + strip + 2] for j in range(frames)])
    windows = windows.reshape(frames, rows * (strip + 2), chan)
    cells = lax.all_to_all(windows, "tm", 0, 0, tiled=True)
    cells = cells.reshape(frames, rows, strip + 2, chan)

    half_rows, half_cols, width = teacher_top.shape[2:]
    half_strip = half_cols // frames
    t_mid = teacher_mid[0, 0].reshape(rows, frames, strip, chan).transpose(1, 0, 2, 3)
    t_mid = t_mid.reshape(frames, rows * strip, chan)
    t_top = teacher_top[0, 0].reshape(half_rows, frames, half_strip, width).transpose(1, 0, 2, 3)
    points = half_rows * half_strip
    t_top = t_top.reshape(frames, points, width)
    t_mid = lax.all_to_all(t_mid, "tm", 0, 0, tiled=True)
    t_top = lax.all_to_all(t_top, "tm", 0, 0, tiled=True)

    above = lax.ppermute(cells[:, rows - 1], "space", [(i, i + 1) for i in range(spaces - 1)])
    below = lax.ppermute(cells[:, 0], "space", [(i + 1, i) for i in range(spaces - 1)])
    padded = jnp.concatenate([above[:, None], cells, below[:, None]], 1)

    conv = lax.conv_general_dilated(
        padded, w_spatial, (1, 1), "VALID", dimension_numbers=numbers, preferred_element_type=F32
    )
    spatial = jax.nn.silu(conv).astype(BF16).reshape(frames, rows * strip, chan)
    back_one = jnp.pad(spatial[:-1], ((1, 0), (0, 0), (0, 0)))
    back_two = jnp.pad(spatial[:-2], ((2, 0), (0, 0), (0, 0)))
    stacked = jnp.concatenate([back_two, back_one, spatial], -1).reshape(-1, 3 * chan)
    temporal = jnp.dot(stacked, w_temporal, preferred_element_type=F32)
    centre = cells[:, :, 1 : strip + 1].reshape(-1, chan)
    mid = (centre.astype(F32) + temporal).astype(BF16)
    diff_mid = (mid.astype(F32) - t_mid.reshape(-1, chan).astype(F32)).astype(BF16)
    scale_mid = 1.0 / math.sqrt(rows * cols * devices_all)
    grad_temporal = (
        lax.dot_general(stacked, diff_mid, (((0,), (0,)), ((), ())), preferred_element_type=F32)
        * scale_mid
    )
    grad_temporal = reduce_shares(grad_temporal)

    coarse = lax.conv_general_dilated(
        mid.reshape(frames, rows, strip, chan),
        w_down,
        (2, 2),
        "VALID",
        dimension_numbers=numbers,
        preferred_element_type=F32,
    ).astype(BF16)
    coarse = coarse.reshape(frames * points, width)
    query = jnp.dot(coarse, w_query, preferred_element_type=F32).astype(BF16)
    key = jnp.dot(coarse, w_key, preferred_element_type=F32).astype(BF16)
    value = jnp.dot(coarse, w_value, preferred_element_type=F32).astype(BF16)
    query = query.astype(F32).reshape(frames, points, width)
    key = key.astype(F32).reshape(frames, points, width)
    value = value.astype(F32).reshape(frames, points, width)
    scores = jnp.sum(query[:, None] * key[None], -1) * (1.0 / math.sqrt(width))
    earlier = jnp.arange(frames)[:, None] >= jnp.arange(frames)[None, :]
    scores = jnp.where(earlier[:, :, None], scores, -1e30)
    best = jnp.max(scores, 1, keepdims=True)
    weights = jnp.where(earlier[:, :, None], jnp.exp(scores - best), 0.0)
    totals = jnp.sum(weights, 1)
    attended = jnp.sum(weights[..., None] * value[None], 1) / totals[..., None]
    attended = attended.astype(BF16).reshape(frames * points, width)
    out = jnp.dot(attended, w_out, preferred_element_type=F32)
    student = (coarse.astype(F32) + out).astype(BF16)
    home = lax.all_to_all(student.reshape(frames, points, width), "tm", 0, 0, tiled=True)
    home = home.reshape(frames, half_rows, half_strip, width).transpose(1, 0, 2, 3)
    diff_top = (student.astype(F32) - t_top.reshape(-1, width).astype(F32)).astype(BF16)
    scale_top = 1.0 / math.sqrt(points * frames * devices_all)
    grad_out = (
        lax.dot_general(attended, diff_top, (((0,), (0,)), ((), ())), preferred_element_type=F32)
        * scale_top
    )
    grad_out = reduce_shares(grad_out)
    return (home.reshape(1, 1, half_rows, half_cols, width), grad_temporal, grad_out)


def solution(mesh):
    return jax.shard_map(
        local,
        mesh=mesh,
        in_specs=(
            P("dp", "tm", "space", None, None),
            P(),
            P(),
            P("dp", "tm", "space", None, None),
            P(),
            P(),
            P(),
            P(),
            P(),
            P("dp", "tm", "space", None, None),
        ),
        out_specs=(
            P("dp", "tm", "space", None, None),
            P(("tm", "space"), None),
            P(("tm", "space"), None),
        ),
        check_vma=False,
    )
```

```python
import functools
import math

import jax
import jax.numpy as jnp
import numpy as np
from jax import lax
from jax.experimental import pallas as pl
from jax.experimental.pallas import tpu as pltpu
from jax.sharding import PartitionSpec as P

F32 = jnp.float32
BF16 = jnp.bfloat16
NEG = -1e30


def call(body, out_shape, args, any_args=(), scratch=(), name=None):
    specs = [
        pl.BlockSpec(memory_space=pl.ANY if i in any_args else pltpu.VMEM)
        for i in range(len(args))
    ]
    outs = [pl.BlockSpec(memory_space=pltpu.VMEM) for _ in out_shape]
    return pl.pallas_call(
        body,
        out_shape=out_shape,
        in_specs=specs,
        out_specs=outs,
        scratch_shapes=list(scratch),
        compiler_params=pltpu.CompilerParams(vmem_limit_bytes=48 << 20),
        name=name,
    )(*args)


def place():
    index = lax.axis_index("tm")
    return index // 2, index % 2


def edge_picker(count, cols, strip):
    strips = cols // strip
    pick = np.zeros((strips, 2 * 8, count * cols), np.float32)
    for j in range(strips):
        for r in range(count):
            if j > 0:
                pick[j, r, r * cols + j * strip - 1] = 1
            if j < strips - 1:
                pick[j, count + r, r * cols + (j + 1) * strip] = 1
    return jnp.asarray(pick.reshape(strips * 16, count * cols), BF16)


def pack_cells_body(own, partner, pick, *refs, links):
    outs, edges = refs[:links], refs[links]
    zhi, core = place()
    count, cols, chan = own.shape
    strip = cols // (2 * links)
    for s, source in enumerate((own, partner)):
        flat = source[...].reshape(count * cols, chan)
        found = jnp.dot(pick[...], flat, preferred_element_type=F32).astype(BF16)
        edges[...] = found.reshape(2 * links, 16, chan)
        for k in range(links):
            j = 2 * lax.rem(zhi + k, links) + core
            begin = pl.multiple_of(j * strip, strip)
            piece = source[:, pl.ds(begin, strip), :].reshape(count * strip, chan)
            outs[k][s, : count * strip] = piece
            outs[k][s, count * strip :] = edges[j]


def pack_cells(own, partner, links):
    count, cols, chan = own.shape
    strip = cols // (2 * links)
    pick = edge_picker(count, cols, strip)
    shape = jax.ShapeDtypeStruct((2, count * strip + 16, chan), BF16)
    return call(
        functools.partial(pack_cells_body, links=links),
        [shape] * links,
        (own, partner, pick),
        scratch=[pltpu.VMEM((2 * links, 16, chan), BF16)],
        name="pack_cells",
    )


def pack_teacher_body(own_mid, partner_mid, own_top, partner_top, *outs, links):
    zhi, core = place()
    rows, cols, chan = own_mid.shape
    half_rows, half_cols, width = own_top.shape
    strip = cols // (2 * links)
    half = half_cols // (2 * links)
    base = rows * strip
    points = half_rows * half
    for k in range(links):
        dest = lax.rem(zhi + k, links)
        j = 2 * dest + core
        for s, (mid, top) in enumerate(((own_mid, own_top), (partner_mid, partner_top))):
            begin = pl.multiple_of(j * strip, strip)
            outs[k][s, :base] = mid[:, pl.ds(begin, strip), :].reshape(base, chan)
            begin = pl.multiple_of(dest * 2 * half, 2 * half)
            both = top[:, pl.ds(begin, 2 * half), :].astype(F32)
            mine = jnp.where(core == 0, both[:, :half], both[:, half:])
            mine = mine.reshape(points, width)
            outs[k][s, base : base + points] = mine[:, :chan].astype(BF16)
            outs[k][s, base + points :] = mine[:, chan:].astype(BF16)


def pack_teacher(own_mid, partner_mid, own_top, partner_top, links):
    rows, cols, chan = own_mid.shape
    half_rows, half_cols, width = own_top.shape
    points = half_rows * (half_cols // (2 * links))
    height = rows * (cols // (2 * links)) + points * (width // chan)
    shape = jax.ShapeDtypeStruct((2, height, chan), BF16)
    return call(
        functools.partial(pack_teacher_body, links=links),
        [shape] * links,
        (own_mid, partner_mid, own_top, partner_top),
        name="pack_teacher",
    )


def shift_pickers(rows, strip):
    main = rows * strip
    left = np.zeros((rows + 2, strip, main + 16 + 2 * strip + 16), np.float32)
    right = np.zeros_like(left)
    halo = main + 16
    corner = halo + 2 * strip
    for q in range(rows + 2):
        if q == 0:
            cell, l_edge, r_edge = halo, corner, corner + 2
        elif q == rows + 1:
            cell, l_edge, r_edge = halo + strip, corner + 1, corner + 3
        else:
            cell, l_edge, r_edge = (q - 1) * strip, main + q - 1, main + rows + q - 1
        for c in range(strip):
            left[q, c, cell + c - 1 if c > 0 else l_edge] = 1
            right[q, c, cell + c + 1 if c < strip - 1 else r_edge] = 1
    both = np.concatenate([left, right], 0).reshape(2 * (rows + 2) * strip, -1)
    return jnp.asarray(both, BF16)


def parity_picker(frames, strip):
    half = strip // 2
    pick = np.zeros((2, frames, half, frames, strip), np.float32)
    for b in range(2):
        for t in range(frames):
            for c in range(half):
                pick[b, t, c, t, 2 * c + b] = 1
    return jnp.asarray(pick.reshape(frames * strip, frames * strip), BF16)


def encode_body(*refs, links, rows, strip):
    cells, refs = refs[:links], refs[links:]
    halos, refs = refs[:links], refs[links:]
    shifts, parity, w_spatial, w_temporal_h, w_down_h, w_proj_h, refs = (*refs[:6], refs[6:])
    spatial, mid_out, attended_out, student_out, refs = (*refs[:4], refs[4:])
    pieces, refs = refs[:links], refs[links:]
    grid, cat, patch, top, w_temporal, w_down, w_proj, sems = refs
    copies = [
        pltpu.make_async_copy(w_temporal_h, w_temporal, sems.at[0]),
        pltpu.make_async_copy(w_down_h, w_down, sems.at[1]),
        pltpu.make_async_copy(w_proj_h, w_proj, sems.at[2]),
    ]
    for copy in copies:
        copy.start()
    zhi, core = place()
    frames = 2 * links
    chan = spatial.shape[-1]
    width = attended_out.shape[-1]
    main = rows * strip
    tall = (rows + 2) * strip
    for k in range(links):
        origin = lax.rem(zhi - k + links, links)
        for s in range(2):
            t = 2 * origin + (core if s == 0 else 1 - core)
            cat[: main + 16] = cells[k][s]
            cat[main + 16 :] = halos[k][s]
            moved = jnp.dot(shifts[...], cat[...], preferred_element_type=F32).astype(BF16)
            grid[:, t, :, :chan] = moved[:tall].reshape(rows + 2, strip, chan)
            grid[:, t, :, 2 * chan :] = moved[tall:].reshape(rows + 2, strip, chan)
            grid[0, t, :, chan : 2 * chan] = halos[k][s, :strip]
            grid[1 : rows + 1, t, :, chan : 2 * chan] = cells[k][s, :main].reshape(
                rows, strip, chan
            )
            grid[rows + 1, t, :, chan : 2 * chan] = halos[k][s, strip : 2 * strip]
    cellcount = rows * frames * strip
    conv = jnp.dot(
        grid[:rows].reshape(cellcount, 3 * chan), w_spatial[0], preferred_element_type=F32
    )
    for d in range(1, 3):
        conv = conv + jnp.dot(
            grid[d : rows + d].reshape(cellcount, 3 * chan),
            w_spatial[d],
            preferred_element_type=F32,
        )
    conv = conv / (1.0 + jnp.exp(-conv))
    spatial[:, :2] = jnp.zeros((rows, 2, strip, chan), BF16)
    spatial[:, 2:] = conv.astype(BF16).reshape(rows, frames, strip, chan)
    copies[0].wait()
    acc = grid[1 : rows + 1, :, :, chan : 2 * chan].reshape(cellcount, chan).astype(F32)
    temporal = jnp.dot(
        spatial[:, :frames].reshape(cellcount, chan),
        w_temporal[:chan],
        preferred_element_type=F32,
    )
    for m in range(1, 3):
        temporal = temporal + jnp.dot(
            spatial[:, m : m + frames].reshape(cellcount, chan),
            w_temporal[m * chan : (m + 1) * chan],
            preferred_element_type=F32,
        )
    mid_out[...] = (acc + temporal).astype(BF16)
    line = frames * strip
    half = strip // 2
    for r in range(rows):
        both = jnp.dot(
            parity[...], mid_out[r * line : (r + 1) * line], preferred_element_type=F32
        ).astype(BF16)
        i, a = r // 2, r % 2
        span = slice(i * line // 2, (i + 1) * line // 2)
        patch[span, 2 * a * chan : (2 * a + 1) * chan] = both[: line // 2]
        patch[span, (2 * a + 1) * chan : (2 * a + 2) * chan] = both[line // 2 :]
    copies[1].wait()
    coarse = jnp.dot(patch[...], w_down[...], preferred_element_type=F32).astype(BF16)
    copies[2].wait()
    half_rows = rows // 2
    quads = (half_rows, frames, half, width)
    query = jnp.dot(coarse, w_proj[0], preferred_element_type=F32).astype(BF16)
    key = jnp.dot(coarse, w_proj[1], preferred_element_type=F32).astype(BF16)
    value = jnp.dot(coarse, w_proj[2], preferred_element_type=F32).astype(BF16)
    top[0] = query.astype(F32).reshape(quads)
    top[1] = key.astype(F32).reshape(quads)
    top[2] = value.astype(F32).reshape(quads)
    scale = 1.0 / math.sqrt(width)

    def attend(i, carry):
        for t in range(frames):
            q = top[0, i, t]
            scores = [
                jnp.sum(q * top[1, i, s], -1, keepdims=True) * scale for s in range(t + 1)
            ]
            best = functools.reduce(jnp.maximum, scores)
            weights = [jnp.exp(score - best) for score in scores]
            total = functools.reduce(jnp.add, weights)
            mix = functools.reduce(
                jnp.add, [weights[s] * top[2, i, s] for s in range(t + 1)]
            )
            top[3, i, t] = mix / total
        return carry

    lax.fori_loop(0, half_rows, attend, 0)
    attended = top[3].reshape(half_rows * frames * half, width).astype(BF16)
    attended_out[...] = attended
    out = jnp.dot(attended, w_proj[3], preferred_element_type=F32)
    student = (coarse.astype(F32) + out).astype(BF16)
    student_out[...] = student
    top[0] = student.astype(F32).reshape(quads)
    for k in range(links):
        dest = lax.rem(zhi + k, links)
        for s in range(2):
            t = 2 * dest + (core if s == 0 else 1 - core)
            pieces[k][s] = top[0, :, t].reshape(half_rows * half, width).astype(BF16)


def encode(cells, halos, w_spatial, w_temporal, w_down, w_proj, links, rows, strip):
    frames = 2 * links
    chan = w_temporal.shape[1]
    width = w_down.shape[-1]
    half = strip // 2
    points = (rows // 2) * half
    args = (
        *cells,
        *halos,
        shift_pickers(rows, strip),
        parity_picker(frames, strip),
        w_spatial.reshape(3, 3 * chan, chan),
        w_temporal,
        w_down.reshape(4 * chan, width),
        w_proj,
    )
    first = 2 * links + 3
    shapes = [
        jax.ShapeDtypeStruct((rows, frames + 2, strip, chan), BF16),
        jax.ShapeDtypeStruct((rows * frames * strip, chan), BF16),
        jax.ShapeDtypeStruct((frames * points, width), BF16),
        jax.ShapeDtypeStruct((frames * points, width), BF16),
    ] + [jax.ShapeDtypeStruct((2, points, width), BF16)] * links
    scratch = [
        pltpu.VMEM((rows + 2, frames, strip, 3 * chan), BF16),
        pltpu.VMEM((rows * strip + 16 + 2 * strip + 16, chan), BF16),
        pltpu.VMEM((frames * points, 4 * chan), BF16),
        pltpu.VMEM((4, rows // 2, frames, half, width), F32),
        pltpu.VMEM(w_temporal.shape, BF16),
        pltpu.VMEM((4 * chan, width), BF16),
        pltpu.VMEM((4, width, width), BF16),
        pltpu.SemaphoreType.DMA((3,)),
    ]
    outs = call(
        functools.partial(encode_body, links=links, rows=rows, strip=strip),
        shapes,
        args,
        any_args=(first, first + 1, first + 2),
        scratch=scratch,
        name="encode",
    )
    return outs[:4], outs[4:]


def gradients_body(*refs, links, scale_mid, scale_top):
    teachers, refs = refs[:links], refs[links:]
    spatial, mid, attended, student, keep, give, t_mid, t_top, g_mid, g_top = refs
    zhi, core = place()
    rows, padded, strip, chan = spatial.shape
    frames = padded - 2
    half_rows, _, half, width = t_top.shape
    base = rows * strip
    points = half_rows * half
    for k in range(links):
        origin = lax.rem(zhi - k + links, links)
        for s in range(2):
            t = 2 * origin + (core if s == 0 else 1 - core)
            t_mid[:, t] = teachers[k][s, :base].reshape(rows, strip, chan)
            low = teachers[k][s, base : base + points].astype(F32)
            high = teachers[k][s, base + points :].astype(F32)
            t_top[:, t, :, :chan] = low.reshape(half_rows, half, chan)
            t_top[:, t, :, chan:] = high.reshape(half_rows, half, chan)
    count = rows * frames * strip
    diff = (mid[...].astype(F32) - t_mid[...].reshape(count, chan).astype(F32)).astype(BF16)
    dims = (((0,), (0,)), ((), ()))
    for m in range(3):
        g_mid[m * chan : (m + 1) * chan] = (
            lax.dot_general(
                spatial[:, m : m + frames].reshape(count, chan),
                diff,
                dims,
                preferred_element_type=F32,
            )
            * scale_mid
        )
    diff = (
        student[...].astype(F32) - t_top[...].reshape(frames * points, width)
    ).astype(BF16)
    g_top[...] = lax.dot_general(attended[...], diff, dims, preferred_element_type=F32) * scale_top
    spaces = keep.shape[1]
    n_mid = g_mid.shape[0] // (frames * spaces)
    n_top = g_top.shape[0] // (frames * spaces)
    for c in range(2):

        @pl.when(core == c)
        def _():
            for side, ref in ((c, keep), (1 - c, give)):
                for z in range(links):
                    for p in range(spaces):
                        shard = (2 * z + side) * spaces + p
                        ref[z, p, :n_mid] = g_mid[shard * n_mid : (shard + 1) * n_mid].astype(
                            ref.dtype
                        )
                        ref[z, p, n_mid:16] = jnp.zeros((16 - n_mid, chan), ref.dtype)
                        block = g_top[shard * n_top : (shard + 1) * n_top].astype(ref.dtype)
                        ref[z, p, 16 : 16 + n_top] = block[:, :chan]
                        ref[z, p, 16 + n_top :] = block[:, chan:]


def gradients(teachers, spatial, mid, attended, student, links, spaces, scale_mid, scale_top):
    rows, padded, strip, chan = spatial.shape
    frames = padded - 2
    width = attended.shape[-1]
    height = 16 + (width // (frames * spaces)) * (width // chan)
    return call(
        functools.partial(
            gradients_body, links=links, scale_mid=scale_mid, scale_top=scale_top
        ),
        [
            jax.ShapeDtypeStruct((links, spaces, height, chan), F32),
            jax.ShapeDtypeStruct((links, spaces, height, chan), F32),
        ],
        (*teachers, spatial, mid, attended, student),
        scratch=[
            pltpu.VMEM((rows, frames, strip, chan), BF16),
            pltpu.VMEM((rows // 2, frames, strip // 2, width), F32),
            pltpu.VMEM((3 * chan, chan), F32),
            pltpu.VMEM((width, width), F32),
        ],
        name="gradients",
    )


def unpack_body(*refs, links):
    mine, swapped, out = refs[:links], refs[links], refs[links + 1]
    zhi, core = place()
    half_rows, cols, width = out.shape
    half = cols // (2 * links)
    for k in range(links):
        origin = lax.rem(zhi - k + links, links)
        own = mine[k][0].astype(F32).reshape(half_rows, half, width)
        other = swapped[k].astype(F32).reshape(half_rows, half, width)
        first = jnp.where(core == 0, own, other)
        second = jnp.where(core == 0, other, own)
        begin = pl.multiple_of(origin * 2 * half, 2 * half)
        out[:, pl.ds(begin, 2 * half), :] = jnp.concatenate([first, second], 1).astype(BF16)


def local(
    feats, w_spatial, w_temporal, teacher_mid, w_down, w_query, w_key, w_value, w_out, teacher_top
):
    frames = lax.axis_size("tm")
    spaces = lax.axis_size("space")
    clips = lax.axis_size("dp")
    links = frames // 2
    devices_all = clips * frames * spaces
    own = feats[0, 0]
    rows, cols, chan = own.shape
    strip = cols // frames
    half_rows, half_cols, width = teacher_top.shape[2:]
    points = half_rows * (half_cols // frames)

    def swap(block):
        return lax.ppermute(block, "tm", [(i, i ^ 1) for i in range(frames)])

    def spread(pieces):
        return [pieces[0]] + [
            lax.ppermute(pieces[k], "tm", [(i, (i + 2 * k) % frames) for i in range(frames)])
            for k in range(1, links)
        ]

    above = lax.ppermute(own[rows - 1], "space", [(i, i + 1) for i in range(spaces - 1)])
    below = lax.ppermute(own[0], "space", [(i + 1, i) for i in range(spaces - 1)])
    cells = spread(pack_cells(own, swap(own), links))
    halo = jnp.stack([above, below])
    halos = spread(pack_cells(halo, swap(halo), links))
    t_mid, t_top = teacher_mid[0, 0], teacher_top[0, 0]
    teachers = spread(pack_teacher(t_mid, swap(t_mid), t_top, swap(t_top), links))

    w_proj = jnp.stack([w_query, w_key, w_value, w_out])
    saved, pieces = encode(
        cells, halos, w_spatial, w_temporal, w_down, w_proj, links, rows, strip
    )
    returned = spread(pieces)
    swapped = swap(jnp.stack([piece[1] for piece in returned]))
    home = call(
        functools.partial(unpack_body, links=links),
        [jax.ShapeDtypeStruct((half_rows, half_cols, width), BF16)],
        (*returned, swapped),
        name="unpack",
    )[0]

    keep, give = gradients(
        teachers,
        *saved,
        links,
        spaces,
        1.0 / math.sqrt(rows * cols * devices_all),
        1.0 / math.sqrt(points * frames * devices_all),
    )
    part = (keep + swap(give)).astype(BF16)
    height = part.shape[2]
    part = part.reshape(links * spaces, height, chan)
    groups = [
        [(2 * z + c) * spaces + p for z in range(links) for p in range(spaces)] for c in range(2)
    ]
    part = lax.all_to_all(
        part, ("tm", "space"), 0, 0, axis_index_groups=groups, tiled=True
    )
    part = jnp.sum(part.astype(F32), 0)
    others = [
        lax.ppermute(part, "dp", [(i, (i + k) % clips) for i in range(clips)])
        for k in range(1, clips)
    ]
    for other in others:
        part = part + other
    n_top = width // (frames * spaces)
    grad_temporal = part[: 3 * chan // (frames * spaces)]
    grad_out = jnp.concatenate([part[16 : 16 + n_top], part[16 + n_top :]], 1)
    return (home[None, None], grad_temporal, grad_out)


def solution(mesh):
    return jax.shard_map(
        local,
        mesh=mesh,
        in_specs=(
            P("dp", "tm", "space", None, None),
            P(),
            P(),
            P("dp", "tm", "space", None, None),
            P(),
            P(),
            P(),
            P(),
            P(),
            P("dp", "tm", "space", None, None),
        ),
        out_specs=(
            P("dp", "tm", "space", None, None),
            P(("tm", "space"), None),
            P(("tm", "space"), None),
        ),
        check_vma=False,
    )
```

```python
import functools
import math

import jax
import jax.numpy as jnp
import numpy as np
from jax import lax
from jax.experimental import pallas as pl
from jax.experimental.pallas import tpu as pltpu
from jax.sharding import PartitionSpec as P


F32 = jnp.float32
BF16 = jnp.bfloat16


def call(body, out_shape, args, scratch=(), room=8, manual=()):
    specs = [
        pl.BlockSpec(memory_space=pltpu.HBM if i in manual else pltpu.VMEM)
        for i in range(len(args))
    ]
    outs = [pl.BlockSpec(memory_space=pltpu.VMEM) for _ in out_shape]
    held = [pltpu.VMEM(args[i].shape, args[i].dtype) for i in manual]

    def run(*refs):
        ins, rest = list(refs[: len(args)]), refs[len(args) :]
        waits = []
        if manual:
            rest, local_refs, sems = rest[: -len(manual) - 1], rest[-len(manual) - 1 : -1], rest[-1]
            for n, i in enumerate(manual):
                copy = pltpu.make_async_copy(ins[i], local_refs[n], sems.at[n])
                copy.start()
                waits.append(copy.wait)
                ins[i] = local_refs[n]
            body(waits, *ins, *rest)
        else:
            body(*ins, *rest)

    extra = held + [pltpu.SemaphoreType.DMA((len(manual),))] if manual else []
    return pl.pallas_call(
        run,
        out_shape=out_shape,
        in_specs=specs,
        out_specs=outs,
        scratch_shapes=[*scratch, *extra],
        compiler_params=pltpu.CompilerParams(vmem_limit_bytes=room << 20),
    )(
        *[
            pltpu.with_memory_space_constraint(arg, pltpu.HBM) if i in manual else arg
            for i, arg in enumerate(args)
        ]
    )


def place():
    index = lax.axis_index("tm")
    return index // 2, index % 2


EDGES = 16


def edge_picker(count, cols, strip):
    strips = cols // strip
    pick = np.zeros((strips, EDGES, count * cols), np.float32)
    for j in range(strips):
        for r in range(count):
            if j > 0:
                pick[j, r, r * cols + j * strip - 1] = 1
            if j < strips - 1:
                pick[j, count + r, r * cols + (j + 1) * strip] = 1
    return jnp.asarray(pick.reshape(strips * EDGES, count * cols), BF16)


def pack_piece(tall, edges, out, s, j):
    count, cols, chan = tall.shape
    strip = cols // edges.shape[0]
    begin = pl.multiple_of(j * strip, strip)
    out[s, : count * strip] = tall[:, pl.ds(begin, strip), :].reshape(count * strip, chan)
    out[s, count * strip :] = edges[j]


def find_edges(tall, pick, edges):
    count, cols, chan = tall.shape
    flat = tall[...].reshape(count * cols, chan)
    found = jnp.dot(pick[...], flat, preferred_element_type=F32).astype(BF16)
    edges[...] = found.reshape(edges.shape)


def pack_main_body(waits, own, partner, pick, out, edges, *, links):
    _, core = place()
    for wait in waits:
        wait()
    for s, source in enumerate((own, partner)):
        find_edges(source, pick, edges)
        for k in range(links):
            pack_piece(source, edges, out.at[k], s, 2 * k + core)


def pack_main(own, partner, links):
    rows, cols, chan = own.shape
    strip = cols // (2 * links)
    return call(
        functools.partial(pack_main_body, links=links),
        [jax.ShapeDtypeStruct((links, 2, rows * strip + EDGES, chan), BF16)],
        (own, partner, edge_picker(rows, cols, strip)),
        scratch=[pltpu.VMEM((2 * links, EDGES, chan), BF16)],
        manual=(0, 2),
    )[0]


def pack_halo_body(waits, *refs, links):
    sources, pick, outs = (refs[:2], refs[2:4]), refs[4], refs[5 : 5 + links]
    tall, edges = refs[5 + links :]
    zhi, core = place()
    for wait in waits:
        wait()
    index = lax.axis_index("space")
    first, last = index == 0, index == lax.axis_size("space") - 1
    for s, (above, below) in enumerate(sources):
        tall[0] = jnp.where(first, jnp.zeros_like(above), above[...])
        tall[1] = jnp.where(last, jnp.zeros_like(below), below[...])
        find_edges(tall, pick, edges)
        for k in range(links):
            pack_piece(tall, edges, outs[k], s, 2 * lax.rem(zhi + k, links) + core)


def pack_halo(own, partner, links):
    cols, chan = own[0].shape
    strip = cols // (2 * links)
    shape = jax.ShapeDtypeStruct((2, 2 * strip + EDGES, chan), BF16)
    return call(
        functools.partial(pack_halo_body, links=links),
        [shape] * links,
        (*own, *partner, edge_picker(2, cols, strip)),
        scratch=[
            pltpu.VMEM((2, cols, chan), BF16),
            pltpu.VMEM((2 * links, EDGES, chan), BF16),
        ],
        manual=(4,),
    )


def pack_teacher_body(waits, own_mid, partner_mid, own_top, partner_top, *outs, links):
    zhi, core = place()
    for wait in waits:
        wait()
    rows, cols, chan = own_mid.shape
    half_rows, half_cols, width = own_top.shape
    strip = cols // (2 * links)
    half = half_cols // (2 * links)
    base = rows * strip
    points = half_rows * half
    for k in range(links):
        dest = lax.rem(zhi + k, links)
        j = 2 * dest + core
        for s, (mid, top) in enumerate(((own_mid, own_top), (partner_mid, partner_top))):
            begin = pl.multiple_of(j * strip, strip)
            outs[k][s, :base] = mid[:, pl.ds(begin, strip), :].reshape(base, chan)
            begin = pl.multiple_of(dest * 2 * half, 2 * half)
            both = top[:, pl.ds(begin, 2 * half), :].astype(F32)
            mine = jnp.where(core == 0, both[:, :half], both[:, half:])
            mine = mine.reshape(points, width)
            outs[k][s, base : base + points] = mine[:, :chan].astype(BF16)
            outs[k][s, base + points :] = mine[:, chan:].astype(BF16)


def pack_teacher(own_mid, partner_mid, own_top, partner_top, links):
    rows, cols, chan = own_mid.shape
    half_rows, half_cols, width = own_top.shape
    points = half_rows * (half_cols // (2 * links))
    height = rows * (cols // (2 * links)) + points * (width // chan)
    return call(
        functools.partial(pack_teacher_body, links=links),
        [jax.ShapeDtypeStruct((2, height, chan), BF16)] * links,
        (own_mid, partner_mid, own_top, partner_top),
        manual=(0, 2),
    )


def shift_pickers(rows, strip):
    main = rows * strip
    halo = main + EDGES
    corner = halo + 2 * strip
    left = np.zeros((rows + 2, strip, corner + EDGES), np.float32)
    right = np.zeros_like(left)
    for q in range(rows + 2):
        if q == 0:
            cell, l_edge, r_edge = halo, corner, corner + 2
        elif q == rows + 1:
            cell, l_edge, r_edge = halo + strip, corner + 1, corner + 3
        else:
            cell, l_edge, r_edge = (q - 1) * strip, main + q - 1, main + rows + q - 1
        for c in range(strip):
            left[q, c, cell + c - 1 if c > 0 else l_edge] = 1
            right[q, c, cell + c + 1 if c < strip - 1 else r_edge] = 1
    both = np.concatenate([left, right], 0).reshape(2 * (rows + 2) * strip, -1)
    return jnp.asarray(both, BF16)


def parity_picker(frames, strip):
    half = strip // 2
    pick = np.zeros((2, frames, half, frames, strip), np.float32)
    for b in range(2):
        for t in range(frames):
            for c in range(half):
                pick[b, t, c, t, 2 * c + b] = 1
    return jnp.asarray(pick.reshape(frames * strip, frames * strip), BF16)


def encode_body(waits, *refs, links, rows, strip):
    cells, shifts, w_spatial, parity, w_temporal, w_down, refs = (*refs[:6], refs[6:])
    halos, refs = refs[:links], refs[links:]
    w_proj, refs = refs[:4], refs[4:]
    spatial, mid_out, attended_out, student_out, refs = (*refs[:4], refs[4:])
    pieces, refs = refs[:links], refs[links:]
    grid, cat, patch, top = refs
    zhi, core = place()
    frames = 2 * links
    chan = spatial.shape[-1]
    width = attended_out.shape[-1]
    tall = (rows + 2) * strip
    waits[0]()
    waits[1]()
    main = rows * strip
    for k in range(links):
        origin = lax.rem(zhi - k + links, links)
        for s in range(2):
            t = 2 * origin + (core if s == 0 else 1 - core)
            cat[: main + EDGES] = cells[origin, s]
            cat[main + EDGES :] = halos[k][s]
            moved = jnp.dot(shifts[...], cat[...], preferred_element_type=F32).astype(BF16)
            grid[:, t, :, :chan] = moved[:tall].reshape(rows + 2, strip, chan)
            grid[:, t, :, 2 * chan :] = moved[tall:].reshape(rows + 2, strip, chan)
            centre = slice(chan, 2 * chan)
            grid[0, t, :, centre] = halos[k][s, :strip]
            grid[1 : rows + 1, t, :, centre] = cells[origin, s, :main].reshape(rows, strip, chan)
            grid[rows + 1, t, :, centre] = halos[k][s, strip : 2 * strip]
    waits[2]()
    cellcount = rows * frames * strip
    conv = jnp.dot(
        grid[:rows].reshape(cellcount, 3 * chan), w_spatial[0], preferred_element_type=F32
    )
    for d in range(1, 3):
        conv = conv + jnp.dot(
            grid[d : rows + d].reshape(cellcount, 3 * chan),
            w_spatial[d],
            preferred_element_type=F32,
        )
    conv = conv / (1.0 + jnp.exp(-conv))
    spatial[:, :2] = jnp.zeros((rows, 2, strip, chan), BF16)
    spatial[:, 2:] = conv.astype(BF16).reshape(rows, frames, strip, chan)
    for wait in waits[3:]:
        wait()
    acc = grid[1 : rows + 1, :, :, chan : 2 * chan].reshape(cellcount, chan).astype(F32)
    temporal = jnp.dot(
        spatial[:, :frames].reshape(cellcount, chan),
        w_temporal[:chan],
        preferred_element_type=F32,
    )
    for m in range(1, 3):
        temporal = temporal + jnp.dot(
            spatial[:, m : m + frames].reshape(cellcount, chan),
            w_temporal[m * chan : (m + 1) * chan],
            preferred_element_type=F32,
        )
    mid_out[...] = (acc + temporal).astype(BF16)
    line = frames * strip
    half = strip // 2
    for r in range(rows):
        both = jnp.dot(
            parity[...], mid_out[r * line : (r + 1) * line], preferred_element_type=F32
        ).astype(BF16)
        i, a = r // 2, r % 2
        span = slice(i * line // 2, (i + 1) * line // 2)
        patch[span, 2 * a * chan : (2 * a + 1) * chan] = both[: line // 2]
        patch[span, (2 * a + 1) * chan : (2 * a + 2) * chan] = both[line // 2 :]
    coarse = jnp.dot(patch[...], w_down[...], preferred_element_type=F32).astype(BF16)
    half_rows = rows // 2
    quads = (half_rows, frames, half, width)
    query = jnp.dot(coarse, w_proj[0][...], preferred_element_type=F32).astype(BF16)
    key = jnp.dot(coarse, w_proj[1][...], preferred_element_type=F32).astype(BF16)
    value = jnp.dot(coarse, w_proj[2][...], preferred_element_type=F32).astype(BF16)
    top[0] = query.astype(F32).reshape(quads)
    top[1] = key.astype(F32).reshape(quads)
    top[2] = value.astype(F32).reshape(quads)
    scale = 1.0 / math.sqrt(width)

    def attend(i, carry):
        for t in range(frames):
            q = top[0, i, t]
            scores = [
                jnp.sum(q * top[1, i, s], -1, keepdims=True) * scale for s in range(t + 1)
            ]
            best = functools.reduce(jnp.maximum, scores)
            weights = [jnp.exp(score - best) for score in scores]
            total = functools.reduce(jnp.add, weights)
            mix = functools.reduce(
                jnp.add, [weights[s] * top[2, i, s] for s in range(t + 1)]
            )
            top[3, i, t] = mix / total
        return carry

    lax.fori_loop(0, half_rows, attend, 0)
    attended = top[3].reshape(half_rows * frames * half, width).astype(BF16)
    attended_out[...] = attended
    out = jnp.dot(attended, w_proj[3][...], preferred_element_type=F32)
    student = (coarse.astype(F32) + out).astype(BF16)
    student_out[...] = student
    top[0] = student.astype(F32).reshape(quads)
    for k in range(links):
        dest = lax.rem(zhi + k, links)
        for s in range(2):
            t = 2 * dest + (core if s == 0 else 1 - core)
            pieces[k][s] = top[0, :, t].reshape(half_rows * half, width).astype(BF16)


def encode(cells, halos, w_spatial, w_temporal, w_down, w_proj, links, rows, strip):
    frames = 2 * links
    chan = w_temporal.shape[1]
    width = w_down.shape[-1]
    half = strip // 2
    points = (rows // 2) * half
    args = (
        cells,
        shift_pickers(rows, strip),
        w_spatial.reshape(3, 3 * chan, chan),
        parity_picker(frames, strip),
        w_temporal,
        w_down.reshape(4 * chan, width),
        *halos,
        *w_proj,
    )
    shapes = [
        jax.ShapeDtypeStruct((rows, frames + 2, strip, chan), BF16),
        jax.ShapeDtypeStruct((rows * frames * strip, chan), BF16),
        jax.ShapeDtypeStruct((frames * points, width), BF16),
        jax.ShapeDtypeStruct((frames * points, width), BF16),
    ] + [jax.ShapeDtypeStruct((2, points, width), BF16)] * links
    scratch = [
        pltpu.VMEM((rows + 2, frames, strip, 3 * chan), BF16),
        pltpu.VMEM((rows * strip + 2 * strip + 2 * EDGES, chan), BF16),
        pltpu.VMEM((frames * points, 4 * chan), BF16),
        pltpu.VMEM((4, rows // 2, frames, half, width), F32),
    ]
    outs = call(
        functools.partial(encode_body, links=links, rows=rows, strip=strip),
        shapes,
        args,
        scratch=scratch,
        room=32,
        manual=(0, 1, 2, 3, 4, 5, *range(6 + links, 10 + links)),
    )
    return outs[:4], outs[4:]


def gradients_body(*refs, links, scale_mid, scale_top):
    teachers, refs = refs[:links], refs[links:]
    spatial, mid, attended, student, keep, give, t_mid, t_top, g_mid, g_top = refs
    zhi, core = place()
    rows, padded, strip, chan = spatial.shape
    frames = padded - 2
    half_rows, _, half, width = t_top.shape
    base = rows * strip
    points = half_rows * half
    for k in range(links):
        origin = lax.rem(zhi - k + links, links)
        for s in range(2):
            t = 2 * origin + (core if s == 0 else 1 - core)
            t_mid[:, t] = teachers[k][s, :base].reshape(rows, strip, chan)
            low = teachers[k][s, base : base + points].astype(F32)
            high = teachers[k][s, base + points :].astype(F32)
            t_top[:, t, :, :chan] = low.reshape(half_rows, half, chan)
            t_top[:, t, :, chan:] = high.reshape(half_rows, half, chan)
    count = rows * frames * strip
    diff = (mid[...].astype(F32) - t_mid[...].reshape(count, chan).astype(F32)).astype(BF16)
    dims = (((0,), (0,)), ((), ()))
    for m in range(3):
        g_mid[m * chan : (m + 1) * chan] = (
            lax.dot_general(
                spatial[:, m : m + frames].reshape(count, chan),
                diff,
                dims,
                preferred_element_type=F32,
            )
            * scale_mid
        )
    diff = (
        student[...].astype(F32) - t_top[...].reshape(frames * points, width)
    ).astype(BF16)
    g_top[...] = lax.dot_general(attended[...], diff, dims, preferred_element_type=F32) * scale_top
    spaces = keep.shape[1]
    n_mid = g_mid.shape[0] // (frames * spaces)
    n_top = g_top.shape[0] // (frames * spaces)
    for c in range(2):

        @pl.when(core == c)
        def _():
            for side, ref in ((c, keep), (1 - c, give)):
                for z in range(links):
                    for p in range(spaces):
                        shard = (2 * z + side) * spaces + p
                        ref[z, p, :n_mid] = g_mid[shard * n_mid : (shard + 1) * n_mid].astype(
                            ref.dtype
                        )
                        ref[z, p, n_mid:16] = jnp.zeros((16 - n_mid, chan), ref.dtype)
                        block = g_top[shard * n_top : (shard + 1) * n_top].astype(ref.dtype)
                        ref[z, p, 16 : 16 + n_top] = block[:, :chan]
                        ref[z, p, 16 + n_top :] = block[:, chan:]


def gradients(teachers, spatial, mid, attended, student, links, spaces, scale_mid, scale_top):
    rows, padded, strip, chan = spatial.shape
    frames = padded - 2
    width = attended.shape[-1]
    height = 16 + (width // (frames * spaces)) * (width // chan)
    return call(
        functools.partial(
            gradients_body, links=links, scale_mid=scale_mid, scale_top=scale_top
        ),
        [
            jax.ShapeDtypeStruct((links, spaces, height, chan), F32),
            jax.ShapeDtypeStruct((links, spaces, height, chan), BF16),
        ],
        (*teachers, spatial, mid, attended, student),
        scratch=[
            pltpu.VMEM((rows, frames, strip, chan), BF16),
            pltpu.VMEM((rows // 2, frames, strip // 2, width), F32),
            pltpu.VMEM((3 * chan, chan), F32),
            pltpu.VMEM((width, width), F32),
        ],
        room=16,
    )


def unpack_body(*refs, links):
    mine, swapped, out = refs[:links], refs[links], refs[links + 1]
    zhi, core = place()
    half_rows, cols, width = out.shape
    half = cols // (2 * links)
    for k in range(links):
        origin = lax.rem(zhi - k + links, links)
        own = mine[k][0].astype(F32).reshape(half_rows, half, width)
        other = swapped[k].astype(F32).reshape(half_rows, half, width)
        first = jnp.where(core == 0, own, other)
        second = jnp.where(core == 0, other, own)
        begin = pl.multiple_of(origin * 2 * half, 2 * half)
        out[:, pl.ds(begin, 2 * half), :] = jnp.concatenate([first, second], 1).astype(BF16)


def finish_body(*refs):
    parts, mid, top = refs[:-2], refs[-2], refs[-1]
    total = functools.reduce(jnp.add, [part[...] for part in parts])
    chan = total.shape[1]
    n_top = top.shape[0]
    mid[...] = total[: mid.shape[0]]
    for h in range(top.shape[1] // chan):
        top[:, h * chan : (h + 1) * chan] = total[16 + h * n_top : 16 + (h + 1) * n_top]


def local(
    feats, w_spatial, w_temporal, teacher_mid, w_down, w_query, w_key, w_value, w_out, teacher_top
):
    frames = lax.axis_size("tm")
    spaces = lax.axis_size("space")
    clips = lax.axis_size("dp")
    links = frames // 2
    devices_all = clips * frames * spaces
    own = feats[0, 0]
    rows, cols, chan = own.shape
    strip = cols // frames
    half_rows, half_cols, width = teacher_top.shape[2:]
    points = half_rows * (half_cols // frames)

    def swap(block):
        return lax.ppermute(block, "tm", [(i, i ^ 1) for i in range(frames)])

    def spread(pieces):
        return [pieces[0]] + [
            lax.ppermute(pieces[k], "tm", [(i, (i + 2 * k) % frames) for i in range(frames)])
            for k in range(1, links)
        ]

    columns = [list(range(c, frames, 2)) for c in range(2)]

    def gather(pieces):
        return lax.all_to_all(pieces, "tm", 0, 0, axis_index_groups=columns, tiled=True)

    ring = [(i, (i + 1) % spaces) for i in range(spaces)]
    above = lax.ppermute(own[rows - 1], "space", ring)
    below = lax.ppermute(own[0], "space", [(j, i) for i, j in ring])
    cells = pack_main(own, swap(own), links)
    cells = gather(cells)
    other = (swap(above), swap(below))
    halo = pack_halo((above, below), other, links)
    halos = spread(halo)
    t_mid, t_top = teacher_mid[0, 0], teacher_top[0, 0]
    teachers = pack_teacher(t_mid, swap(t_mid), t_top, swap(t_top), links)
    teachers = spread(teachers)

    w_proj = (w_query, w_key, w_value, w_out)
    saved, pieces = encode(
        cells, halos, w_spatial, w_temporal, w_down, w_proj, links, rows, strip
    )
    returned = spread(pieces)
    swapped = swap(jnp.stack([piece[1] for piece in returned]))
    home = call(
        functools.partial(unpack_body, links=links),
        [jax.ShapeDtypeStruct((half_rows, half_cols, width), BF16)],
        (*returned, swapped),
    )[0]

    keep, give = gradients(
        teachers,
        *saved,
        links,
        spaces,
        1.0 / math.sqrt(rows * cols * devices_all),
        1.0 / math.sqrt(points * frames * devices_all),
    )
    part = (keep + swap(give).astype(F32)).astype(BF16)
    part = part.reshape(links * spaces, *part.shape[2:])
    groups = [
        [(2 * z + c) * spaces + p for z in range(links) for p in range(spaces)] for c in range(2)
    ]
    part = lax.all_to_all(part, ("tm", "space"), 0, 0, axis_index_groups=groups, tiled=True)
    part = jnp.sum(part.astype(F32), 0)
    others = [
        lax.ppermute(part, "dp", [(i, (i + k) % clips) for i in range(clips)])
        for k in range(1, clips)
    ]
    n_top = width // (frames * spaces)
    grad_temporal, grad_out = call(
        finish_body,
        [
            jax.ShapeDtypeStruct((3 * chan // (frames * spaces), chan), F32),
            jax.ShapeDtypeStruct((n_top, width), F32),
        ],
        (part, *others),
    )
    return (home[None, None], grad_temporal, grad_out)


def solution(mesh):
    return jax.shard_map(
        local,
        mesh=mesh,
        in_specs=(
            P("dp", "tm", "space", None, None),
            P(),
            P(),
            P("dp", "tm", "space", None, None),
            P(),
            P(),
            P(),
            P(),
            P(),
            P("dp", "tm", "space", None, None),
        ),
        out_specs=(
            P("dp", "tm", "space", None, None),
            P(("tm", "space"), None),
            P(("tm", "space"), None),
        ),
        check_vma=False,
    )
```

```python
import functools
import math

import jax
import jax.numpy as jnp
import numpy as np
from jax import lax
from jax.experimental import pallas as pl
from jax.experimental.pallas import tpu as pltpu
from jax.sharding import PartitionSpec as P


F32 = jnp.float32
BF16 = jnp.bfloat16


def call(body, out_shape, args, scratch=(), room=8, manual=()):
    specs = [
        pl.BlockSpec(memory_space=pltpu.HBM if i in manual else pltpu.VMEM)
        for i in range(len(args))
    ]
    outs = [pl.BlockSpec(memory_space=pltpu.VMEM) for _ in out_shape]
    held = [pltpu.VMEM(args[i].shape, args[i].dtype) for i in manual]

    def run(*refs):
        ins, rest = list(refs[: len(args)]), refs[len(args) :]
        waits = []
        if manual:
            rest, local_refs, sems = rest[: -len(manual) - 1], rest[-len(manual) - 1 : -1], rest[-1]
            for n, i in enumerate(manual):
                copy = pltpu.make_async_copy(ins[i], local_refs[n], sems.at[n])
                copy.start()
                waits.append(copy.wait)
                ins[i] = local_refs[n]
            body(waits, *ins, *rest)
        else:
            body(*ins, *rest)

    extra = held + [pltpu.SemaphoreType.DMA((len(manual),))] if manual else []
    return pl.pallas_call(
        run,
        out_shape=out_shape,
        in_specs=specs,
        out_specs=outs,
        scratch_shapes=[*scratch, *extra],
        compiler_params=pltpu.CompilerParams(vmem_limit_bytes=room << 20),
    )(
        *[
            pltpu.with_memory_space_constraint(arg, pltpu.HBM) if i in manual else arg
            for i, arg in enumerate(args)
        ]
    )


def place():
    index = lax.axis_index("tm")
    return index // 2, index % 2


EDGES = 16


def edge_picker(count, cols, strip):
    strips = cols // strip
    pick = np.zeros((strips, EDGES, count * cols), np.float32)
    for j in range(strips):
        for r in range(count):
            if j > 0:
                pick[j, r, r * cols + j * strip - 1] = 1
            if j < strips - 1:
                pick[j, count + r, r * cols + (j + 1) * strip] = 1
    return jnp.asarray(pick.reshape(strips * EDGES, count * cols), BF16)


def pack_piece(tall, edges, out, s, j):
    count, cols, chan = tall.shape
    strip = cols // edges.shape[0]
    begin = pl.multiple_of(j * strip, strip)
    out[s, : count * strip] = tall[:, pl.ds(begin, strip), :].reshape(count * strip, chan)
    out[s, count * strip :] = edges[j]


def find_edges(tall, pick, edges):
    count, cols, chan = tall.shape
    flat = tall[...].reshape(count * cols, chan)
    found = jnp.dot(pick[...], flat, preferred_element_type=F32).astype(BF16)
    edges[...] = found.reshape(edges.shape)


def pack_main_body(waits, own, partner, pick, *refs, links):
    outs, edges = refs[:links], refs[links]
    zhi, core = place()
    for wait in waits:
        wait()
    for s, source in enumerate((own, partner)):
        find_edges(source, pick, edges)
        for k in range(links):
            pack_piece(source, edges, outs[k], s, 2 * lax.rem(zhi + k, links) + core)


def pack_main(own, partner, links):
    rows, cols, chan = own.shape
    strip = cols // (2 * links)
    return call(
        functools.partial(pack_main_body, links=links),
        [jax.ShapeDtypeStruct((2, rows * strip + EDGES, chan), BF16)] * links,
        (own, partner, edge_picker(rows, cols, strip)),
        scratch=[pltpu.VMEM((2 * links, EDGES, chan), BF16)],
        manual=(0, 2),
    )


def pack_halo_body(waits, *refs, links):
    sources, pick, out = (refs[:2], refs[2:4]), refs[4], refs[5]
    tall, edges = refs[6:]
    _, core = place()
    for wait in waits:
        wait()
    index = lax.axis_index("space")
    first, last = index == 0, index == lax.axis_size("space") - 1
    for s, (above, below) in enumerate(sources):
        tall[0] = jnp.where(first, jnp.zeros_like(above), above[...])
        tall[1] = jnp.where(last, jnp.zeros_like(below), below[...])
        find_edges(tall, pick, edges)
        for k in range(links):
            pack_piece(tall, edges, out.at[k], s, 2 * k + core)


def pack_halo(own, partner, links):
    cols, chan = own[0].shape
    strip = cols // (2 * links)
    return call(
        functools.partial(pack_halo_body, links=links),
        [jax.ShapeDtypeStruct((links, 2, 2 * strip + EDGES, chan), BF16)],
        (*own, *partner, edge_picker(2, cols, strip)),
        scratch=[
            pltpu.VMEM((2, cols, chan), BF16),
            pltpu.VMEM((2 * links, EDGES, chan), BF16),
        ],
        manual=(4,),
    )[0]


def pack_teacher_body(waits, own_mid, partner_mid, own_top, partner_top, *outs, links):
    zhi, core = place()
    for wait in waits:
        wait()
    rows, cols, chan = own_mid.shape
    half_rows, half_cols, width = own_top.shape
    strip = cols // (2 * links)
    half = half_cols // (2 * links)
    base = rows * strip
    points = half_rows * half
    for k in range(links):
        dest = lax.rem(zhi + k, links)
        j = 2 * dest + core
        for s, (mid, top) in enumerate(((own_mid, own_top), (partner_mid, partner_top))):
            begin = pl.multiple_of(j * strip, strip)
            outs[k][s, :base] = mid[:, pl.ds(begin, strip), :].reshape(base, chan)
            begin = pl.multiple_of(dest * 2 * half, 2 * half)
            both = top[:, pl.ds(begin, 2 * half), :].astype(F32)
            mine = jnp.where(core == 0, both[:, :half], both[:, half:])
            mine = mine.reshape(points, width)
            outs[k][s, base : base + points] = mine[:, :chan].astype(BF16)
            outs[k][s, base + points :] = mine[:, chan:].astype(BF16)


def pack_teacher(own_mid, partner_mid, own_top, partner_top, links):
    rows, cols, chan = own_mid.shape
    half_rows, half_cols, width = own_top.shape
    points = half_rows * (half_cols // (2 * links))
    height = rows * (cols // (2 * links)) + points * (width // chan)
    return call(
        functools.partial(pack_teacher_body, links=links),
        [jax.ShapeDtypeStruct((2, height, chan), BF16)] * links,
        (own_mid, partner_mid, own_top, partner_top),
        manual=(0, 2),
    )


def shift_pickers(rows, strip):
    main = rows * strip
    halo = main + EDGES
    corner = halo + 2 * strip
    left = np.zeros((rows + 2, strip, corner + EDGES), np.float32)
    right = np.zeros_like(left)
    for q in range(rows + 2):
        if q == 0:
            cell, l_edge, r_edge = halo, corner, corner + 2
        elif q == rows + 1:
            cell, l_edge, r_edge = halo + strip, corner + 1, corner + 3
        else:
            cell, l_edge, r_edge = (q - 1) * strip, main + q - 1, main + rows + q - 1
        for c in range(strip):
            left[q, c, cell + c - 1 if c > 0 else l_edge] = 1
            right[q, c, cell + c + 1 if c < strip - 1 else r_edge] = 1
    both = np.concatenate([left, right], 0).reshape(2 * (rows + 2) * strip, -1)
    return jnp.asarray(both, BF16)


def parity_picker(frames, strip):
    half = strip // 2
    pick = np.zeros((2, frames, half, frames, strip), np.float32)
    for b in range(2):
        for t in range(frames):
            for c in range(half):
                pick[b, t, c, t, 2 * c + b] = 1
    return jnp.asarray(pick.reshape(frames * strip, frames * strip), BF16)


def encode_body(waits, *refs, links, rows, strip):
    halos, shifts, w_spatial, parity, w_temporal, w_down, refs = (*refs[:6], refs[6:])
    cells, refs = refs[:links], refs[links:]
    w_proj, refs = refs[:4], refs[4:]
    spatial, mid_out, attended_out, student_out, refs = (*refs[:4], refs[4:])
    pieces, refs = refs[:links], refs[links:]
    grid, cat, patch, top = refs
    zhi, core = place()
    frames = 2 * links
    chan = spatial.shape[-1]
    width = attended_out.shape[-1]
    tall = (rows + 2) * strip
    waits[0]()
    main = rows * strip
    for k in range(links):
        origin = lax.rem(zhi - k + links, links)
        for s in range(2):
            t = 2 * origin + (core if s == 0 else 1 - core)
            cat[: main + EDGES] = cells[k][s]
            cat[main + EDGES :] = halos[origin, s]
            moved = jnp.dot(shifts[...], cat[...], preferred_element_type=F32).astype(BF16)
            grid[:, t, :, :chan] = moved[:tall].reshape(rows + 2, strip, chan)
            grid[:, t, :, 2 * chan :] = moved[tall:].reshape(rows + 2, strip, chan)
            centre = slice(chan, 2 * chan)
            grid[0, t, :, centre] = halos[origin, s, :strip]
            grid[1 : rows + 1, t, :, centre] = cells[k][s, :main].reshape(rows, strip, chan)
            grid[rows + 1, t, :, centre] = halos[origin, s, strip : 2 * strip]
    waits[1]()
    cellcount = rows * frames * strip
    conv = jnp.dot(
        grid[:rows].reshape(cellcount, 3 * chan), w_spatial[0], preferred_element_type=F32
    )
    for d in range(1, 3):
        conv = conv + jnp.dot(
            grid[d : rows + d].reshape(cellcount, 3 * chan),
            w_spatial[d],
            preferred_element_type=F32,
        )
    conv = conv / (1.0 + jnp.exp(-conv))
    spatial[:, :2] = jnp.zeros((rows, 2, strip, chan), BF16)
    spatial[:, 2:] = conv.astype(BF16).reshape(rows, frames, strip, chan)
    for wait in waits[2:]:
        wait()
    acc = grid[1 : rows + 1, :, :, chan : 2 * chan].reshape(cellcount, chan).astype(F32)
    temporal = jnp.dot(
        spatial[:, :frames].reshape(cellcount, chan),
        w_temporal[:chan],
        preferred_element_type=F32,
    )
    for m in range(1, 3):
        temporal = temporal + jnp.dot(
            spatial[:, m : m + frames].reshape(cellcount, chan),
            w_temporal[m * chan : (m + 1) * chan],
            preferred_element_type=F32,
        )
    mid_out[...] = (acc + temporal).astype(BF16)
    line = frames * strip
    half = strip // 2
    for r in range(rows):
        both = jnp.dot(
            parity[...], mid_out[r * line : (r + 1) * line], preferred_element_type=F32
        ).astype(BF16)
        i, a = r // 2, r % 2
        span = slice(i * line // 2, (i + 1) * line // 2)
        patch[span, 2 * a * chan : (2 * a + 1) * chan] = both[: line // 2]
        patch[span, (2 * a + 1) * chan : (2 * a + 2) * chan] = both[line // 2 :]
    coarse = jnp.dot(patch[...], w_down[...], preferred_element_type=F32).astype(BF16)
    half_rows = rows // 2
    quads = (half_rows, frames, half, width)
    query = jnp.dot(coarse, w_proj[0][...], preferred_element_type=F32).astype(BF16)
    key = jnp.dot(coarse, w_proj[1][...], preferred_element_type=F32).astype(BF16)
    value = jnp.dot(coarse, w_proj[2][...], preferred_element_type=F32).astype(BF16)
    top[0] = query.astype(F32).reshape(quads)
    top[1] = key.astype(F32).reshape(quads)
    top[2] = value.astype(F32).reshape(quads)
    scale = 1.0 / math.sqrt(width)

    def attend(i, carry):
        for t in range(frames):
            q = top[0, i, t]
            scores = [
                jnp.sum(q * top[1, i, s], -1, keepdims=True) * scale for s in range(t + 1)
            ]
            best = functools.reduce(jnp.maximum, scores)
            weights = [jnp.exp(score - best) for score in scores]
            total = functools.reduce(jnp.add, weights)
            mix = functools.reduce(
                jnp.add, [weights[s] * top[2, i, s] for s in range(t + 1)]
            )
            top[3, i, t] = mix / total
        return carry

    lax.fori_loop(0, half_rows, attend, 0)
    attended = top[3].reshape(half_rows * frames * half, width).astype(BF16)
    attended_out[...] = attended
    out = jnp.dot(attended, w_proj[3][...], preferred_element_type=F32)
    student = (coarse.astype(F32) + out).astype(BF16)
    student_out[...] = student
    top[0] = student.astype(F32).reshape(quads)
    for k in range(links):
        dest = lax.rem(zhi + k, links)
        for s in range(2):
            t = 2 * dest + (core if s == 0 else 1 - core)
            pieces[k][s] = top[0, :, t].reshape(half_rows * half, width).astype(BF16)


def encode(cells, halos, w_spatial, w_temporal, w_down, w_proj, links, rows, strip):
    frames = 2 * links
    chan = w_temporal.shape[1]
    width = w_down.shape[-1]
    half = strip // 2
    points = (rows // 2) * half
    args = (
        halos,
        shift_pickers(rows, strip),
        w_spatial.reshape(3, 3 * chan, chan),
        parity_picker(frames, strip),
        w_temporal,
        w_down.reshape(4 * chan, width),
        *cells,
        *w_proj,
    )
    shapes = [
        jax.ShapeDtypeStruct((rows, frames + 2, strip, chan), BF16),
        jax.ShapeDtypeStruct((rows * frames * strip, chan), BF16),
        jax.ShapeDtypeStruct((frames * points, width), BF16),
        jax.ShapeDtypeStruct((frames * points, width), BF16),
    ] + [jax.ShapeDtypeStruct((2, points, width), BF16)] * links
    scratch = [
        pltpu.VMEM((rows + 2, frames, strip, 3 * chan), BF16),
        pltpu.VMEM((rows * strip + 2 * strip + 2 * EDGES, chan), BF16),
        pltpu.VMEM((frames * points, 4 * chan), BF16),
        pltpu.VMEM((4, rows // 2, frames, half, width), F32),
    ]
    outs = call(
        functools.partial(encode_body, links=links, rows=rows, strip=strip),
        shapes,
        args,
        scratch=scratch,
        room=32,
        manual=(1, 2, 3, 4, 5, *range(6 + links, 10 + links)),
    )
    return outs[:4], outs[4:]


def gradients_body(*refs, links, scale_mid, scale_top):
    teachers, refs = refs[:links], refs[links:]
    spatial, mid, attended, student, keep, give, t_mid, t_top, g_mid, g_top = refs
    zhi, core = place()
    rows, padded, strip, chan = spatial.shape
    frames = padded - 2
    half_rows, _, half, width = t_top.shape
    base = rows * strip
    points = half_rows * half
    for k in range(links):
        origin = lax.rem(zhi - k + links, links)
        for s in range(2):
            t = 2 * origin + (core if s == 0 else 1 - core)
            t_mid[:, t] = teachers[k][s, :base].reshape(rows, strip, chan)
            low = teachers[k][s, base : base + points].astype(F32)
            high = teachers[k][s, base + points :].astype(F32)
            t_top[:, t, :, :chan] = low.reshape(half_rows, half, chan)
            t_top[:, t, :, chan:] = high.reshape(half_rows, half, chan)
    count = rows * frames * strip
    diff = (mid[...].astype(F32) - t_mid[...].reshape(count, chan).astype(F32)).astype(BF16)
    dims = (((0,), (0,)), ((), ()))
    for m in range(3):
        g_mid[m * chan : (m + 1) * chan] = (
            lax.dot_general(
                spatial[:, m : m + frames].reshape(count, chan),
                diff,
                dims,
                preferred_element_type=F32,
            )
            * scale_mid
        )
    diff = (
        student[...].astype(F32) - t_top[...].reshape(frames * points, width)
    ).astype(BF16)
    g_top[...] = lax.dot_general(attended[...], diff, dims, preferred_element_type=F32) * scale_top
    spaces = 2 * keep.shape[0]
    n_mid = g_mid.shape[0] // (frames * spaces)
    n_top = g_top.shape[0] // (frames * spaces)
    for c in range(2):

        @pl.when(core == c)
        def _():
            for side, ref in ((c, keep), (1 - c, give)):
                for z in range(links):
                    for p in range(spaces):
                        shard = (2 * z + side) * spaces + p
                        ref[p // 2, z, p % 2, :n_mid] = g_mid[shard * n_mid : (shard + 1) * n_mid].astype(
                            ref.dtype
                        )
                        ref[p // 2, z, p % 2, n_mid:16] = jnp.zeros((16 - n_mid, chan), ref.dtype)
                        block = g_top[shard * n_top : (shard + 1) * n_top].astype(ref.dtype)
                        ref[p // 2, z, p % 2, 16 : 16 + n_top] = block[:, :chan]
                        ref[p // 2, z, p % 2, 16 + n_top :] = block[:, chan:]


def gradients(teachers, spatial, mid, attended, student, links, spaces, scale_mid, scale_top):
    rows, padded, strip, chan = spatial.shape
    frames = padded - 2
    width = attended.shape[-1]
    height = 16 + (width // (frames * spaces)) * (width // chan)
    return call(
        functools.partial(
            gradients_body, links=links, scale_mid=scale_mid, scale_top=scale_top
        ),
        [
            jax.ShapeDtypeStruct((spaces // 2, links, 2, height, chan), F32),
            jax.ShapeDtypeStruct((spaces // 2, links, 2, height, chan), BF16),
        ],
        (*teachers, spatial, mid, attended, student),
        scratch=[
            pltpu.VMEM((rows, frames, strip, chan), BF16),
            pltpu.VMEM((rows // 2, frames, strip // 2, width), F32),
            pltpu.VMEM((3 * chan, chan), F32),
            pltpu.VMEM((width, width), F32),
        ],
        room=16,
    )


def unpack_body(*refs, links):
    mine, swapped, out = refs[:links], refs[links], refs[links + 1]
    zhi, core = place()
    half_rows, cols, width = out.shape
    half = cols // (2 * links)
    for k in range(links):
        origin = lax.rem(zhi - k + links, links)
        own = mine[k][0].astype(F32).reshape(half_rows, half, width)
        other = swapped[k].astype(F32).reshape(half_rows, half, width)
        first = jnp.where(core == 0, own, other)
        second = jnp.where(core == 0, other, own)
        begin = pl.multiple_of(origin * 2 * half, 2 * half)
        out[:, pl.ds(begin, 2 * half), :] = jnp.concatenate([first, second], 1).astype(BF16)


def finish_body(*refs):
    parts, mid, top = refs[:-2], refs[-2], refs[-1]
    total = functools.reduce(jnp.add, [part[...] for part in parts])
    chan = total.shape[1]
    n_top = top.shape[0]
    mid[...] = total[: mid.shape[0]]
    for h in range(top.shape[1] // chan):
        top[:, h * chan : (h + 1) * chan] = total[16 + h * n_top : 16 + (h + 1) * n_top]


def local(
    feats, w_spatial, w_temporal, teacher_mid, w_down, w_query, w_key, w_value, w_out, teacher_top
):
    frames = lax.axis_size("tm")
    spaces = lax.axis_size("space")
    clips = lax.axis_size("dp")
    links = frames // 2
    devices_all = clips * frames * spaces
    own = feats[0, 0]
    rows, cols, chan = own.shape
    strip = cols // frames
    half_rows, half_cols, width = teacher_top.shape[2:]
    points = half_rows * (half_cols // frames)

    def swap(block):
        return lax.ppermute(block, "tm", [(i, i ^ 1) for i in range(frames)])

    def spread(pieces):
        return [pieces[0]] + [
            lax.ppermute(pieces[k], "tm", [(i, (i + 2 * k) % frames) for i in range(frames)])
            for k in range(1, links)
        ]

    columns = [list(range(c, frames, 2)) for c in range(2)]

    def gather(pieces):
        return lax.all_to_all(pieces, "tm", 0, 0, axis_index_groups=columns, tiled=True)

    ring = [(i, (i + 1) % spaces) for i in range(spaces)]
    above = lax.ppermute(own[rows - 1], "space", ring)
    below = lax.ppermute(own[0], "space", [(j, i) for i, j in ring])
    cells = pack_main(own, swap(own), links)
    cells = spread(cells)
    other = (swap(above), swap(below))
    halo = pack_halo((above, below), other, links)
    halos = gather(halo)
    t_mid, t_top = teacher_mid[0, 0], teacher_top[0, 0]
    teachers = pack_teacher(t_mid, swap(t_mid), t_top, swap(t_top), links)
    teachers = spread(teachers)

    w_proj = (w_query, w_key, w_value, w_out)
    saved, pieces = encode(
        cells, halos, w_spatial, w_temporal, w_down, w_proj, links, rows, strip
    )
    returned = spread(pieces)
    swapped = swap(jnp.stack([piece[1] for piece in returned]))
    home = call(
        functools.partial(unpack_body, links=links),
        [jax.ShapeDtypeStruct((half_rows, half_cols, width), BF16)],
        (*returned, swapped),
    )[0]

    keep, give = gradients(
        teachers,
        *saved,
        links,
        spaces,
        1.0 / math.sqrt(rows * cols * devices_all),
        1.0 / math.sqrt(points * frames * devices_all),
    )
    part = (keep + swap(give).astype(F32)).astype(BF16)
    lines = [list(range(a, spaces, 2)) for a in range(2)]
    part = lax.all_to_all(part, "space", 0, 0, axis_index_groups=lines, tiled=True)
    part = jnp.sum(part.astype(F32), 0).astype(BF16)
    part = part.reshape(frames, *part.shape[2:])
    groups = [
        [(2 * z + c) * spaces + p + a for z in range(links) for a in range(2)]
        for c in range(2)
        for p in range(0, spaces, 2)
    ]
    part = lax.all_to_all(part, ("tm", "space"), 0, 0, axis_index_groups=groups, tiled=True)
    part = jnp.sum(part.astype(F32), 0)
    others = [
        lax.ppermute(part, "dp", [(i, (i + k) % clips) for i in range(clips)])
        for k in range(1, clips)
    ]
    n_top = width // (frames * spaces)
    grad_temporal, grad_out = call(
        finish_body,
        [
            jax.ShapeDtypeStruct((3 * chan // (frames * spaces), chan), F32),
            jax.ShapeDtypeStruct((n_top, width), F32),
        ],
        (part, *others),
    )
    return (home[None, None], grad_temporal, grad_out)


def solution(mesh):
    return jax.shard_map(
        local,
        mesh=mesh,
        in_specs=(
            P("dp", "tm", "space", None, None),
            P(),
            P(),
            P("dp", "tm", "space", None, None),
            P(),
            P(),
            P(),
            P(),
            P(),
            P("dp", "tm", "space", None, None),
        ),
        out_specs=(
            P("dp", "tm", "space", None, None),
            P(("tm", "space"), None),
            P(("tm", "space"), None),
        ),
        check_vma=False,
    )
```

```python
import functools
import math

import jax
import jax.numpy as jnp
import numpy as np
from jax import lax
from jax.experimental import pallas as pl
from jax.experimental.pallas import tpu as pltpu
from jax.sharding import PartitionSpec as P


F32 = jnp.float32
BF16 = jnp.bfloat16
LANES = 128


def call(body, out_shape, args, scratch=(), room=8, manual=()):
    specs = [
        pl.BlockSpec(memory_space=pltpu.HBM if i in manual else pltpu.VMEM)
        for i in range(len(args))
    ]
    outs = [pl.BlockSpec(memory_space=pltpu.VMEM) for _ in out_shape]
    held = [pltpu.VMEM(args[i].shape, args[i].dtype) for i in manual]

    def run(*refs):
        ins, rest = list(refs[: len(args)]), refs[len(args) :]
        waits = []
        if manual:
            rest, local_refs, sems = rest[: -len(manual) - 1], rest[-len(manual) - 1 : -1], rest[-1]
            for n, i in enumerate(manual):
                copy = pltpu.make_async_copy(ins[i], local_refs[n], sems.at[n])
                copy.start()
                waits.append(copy.wait)
                ins[i] = local_refs[n]
            body(waits, *ins, *rest)
        else:
            body(*ins, *rest)

    extra = held + [pltpu.SemaphoreType.DMA((len(manual),))] if manual else []
    return pl.pallas_call(
        run,
        out_shape=out_shape,
        in_specs=specs,
        out_specs=outs,
        scratch_shapes=[*scratch, *extra],
        compiler_params=pltpu.CompilerParams(vmem_limit_bytes=room << 20),
    )(
        *[
            pltpu.with_memory_space_constraint(arg, pltpu.HBM) if i in manual else arg
            for i, arg in enumerate(args)
        ]
    )


def place():
    index = lax.axis_index("tm")
    return index // 2, index % 2


EDGES = 16


def edge_picker(count, cols, strip):
    strips = cols // strip
    pick = np.zeros((strips, EDGES, count * cols), np.float32)
    for j in range(strips):
        for r in range(count):
            if j > 0:
                pick[j, r, r * cols + j * strip - 1] = 1
            if j < strips - 1:
                pick[j, count + r, r * cols + (j + 1) * strip] = 1
    return jnp.asarray(pick.reshape(strips * EDGES, count * cols), BF16)


def pack_piece(tall, edges, out, s, j):
    count, cols, chan = tall.shape
    strip = cols // edges.shape[0]
    begin = pl.multiple_of(j * strip, strip)
    out[s, : count * strip] = tall[:, pl.ds(begin, strip), :].reshape(count * strip, chan)
    out[s, count * strip :] = edges[j]


def find_edges(tall, pick, edges):
    count, cols, chan = tall.shape
    flat = tall[...].reshape(count * cols, chan)
    found = jnp.dot(pick[...], flat, preferred_element_type=F32).astype(BF16)
    edges[...] = found.reshape(edges.shape)


def pack_main_body(waits, own, partner, pick, *refs, links):
    outs, edges = refs[:links], refs[links]
    zhi, core = place()
    for wait in waits:
        wait()
    for s, source in enumerate((own, partner)):
        find_edges(source, pick, edges)
        for k in range(links):
            pack_piece(source, edges, outs[k], s, 2 * lax.rem(zhi + k, links) + core)


def pack_main(own, partner, links):
    rows, cols, chan = own.shape
    strip = cols // (2 * links)
    return call(
        functools.partial(pack_main_body, links=links),
        [jax.ShapeDtypeStruct((2, rows * strip + EDGES, chan), BF16)] * links,
        (own, partner, edge_picker(rows, cols, strip)),
        scratch=[pltpu.VMEM((2 * links, EDGES, chan), BF16)],
        manual=(0, 2),
    )


def pack_halo_body(waits, *refs, links):
    sources, pick, out = (refs[:2], refs[2:4]), refs[4], refs[5]
    tall, edges = refs[6:]
    _, core = place()
    for wait in waits:
        wait()
    index = lax.axis_index("space")
    first, last = index == 0, index == lax.axis_size("space") - 1
    for s, (above, below) in enumerate(sources):
        tall[0] = jnp.where(first, jnp.zeros_like(above), above[...])
        tall[1] = jnp.where(last, jnp.zeros_like(below), below[...])
        find_edges(tall, pick, edges)
        for k in range(links):
            pack_piece(tall, edges, out.at[k], s, 2 * k + core)


def pack_halo(own, partner, links):
    cols, chan = own[0].shape
    strip = cols // (2 * links)
    return call(
        functools.partial(pack_halo_body, links=links),
        [jax.ShapeDtypeStruct((links, 2, 2 * strip + EDGES, chan), BF16)],
        (*own, *partner, edge_picker(2, cols, strip)),
        scratch=[
            pltpu.VMEM((2, cols, chan), BF16),
            pltpu.VMEM((2 * links, EDGES, chan), BF16),
        ],
        manual=(4,),
    )[0]


def pack_teacher_body(waits, own_mid, partner_mid, own_top, partner_top, *outs, links):
    zhi, core = place()
    for wait in waits:
        wait()
    rows, cols, chan = own_mid.shape
    half_rows, half_cols, width = own_top.shape
    strip = cols // (2 * links)
    half = half_cols // (2 * links)
    base = rows * strip
    points = half_rows * half
    for k in range(links):
        dest = lax.rem(zhi + k, links)
        j = 2 * dest + core
        for s, (mid, top) in enumerate(((own_mid, own_top), (partner_mid, partner_top))):
            begin = pl.multiple_of(j * strip, strip)
            outs[k][s, :base] = mid[:, pl.ds(begin, strip), :].reshape(base, chan)
            begin = pl.multiple_of(dest * 2 * half, 2 * half)
            both = top[:, pl.ds(begin, 2 * half), :].astype(F32)
            mine = jnp.where(core == 0, both[:, :half], both[:, half:])
            mine = mine.reshape(points, width)
            outs[k][s, base : base + points] = mine[:, :chan].astype(BF16)
            outs[k][s, base + points :] = mine[:, chan:].astype(BF16)


def pack_teacher(own_mid, partner_mid, own_top, partner_top, links):
    rows, cols, chan = own_mid.shape
    half_rows, half_cols, width = own_top.shape
    points = half_rows * (half_cols // (2 * links))
    height = rows * (cols // (2 * links)) + points * (width // chan)
    return call(
        functools.partial(pack_teacher_body, links=links),
        [jax.ShapeDtypeStruct((2, height, chan), BF16)] * links,
        (own_mid, partner_mid, own_top, partner_top),
        manual=(0, 2),
    )


def shift_pickers(rows, strip):
    main = rows * strip
    halo = main + EDGES
    corner = halo + 2 * strip
    left = np.zeros((rows + 2, strip, corner + EDGES), np.float32)
    right = np.zeros_like(left)
    for q in range(rows + 2):
        if q == 0:
            cell, l_edge, r_edge = halo, corner, corner + 2
        elif q == rows + 1:
            cell, l_edge, r_edge = halo + strip, corner + 1, corner + 3
        else:
            cell, l_edge, r_edge = (q - 1) * strip, main + q - 1, main + rows + q - 1
        for c in range(strip):
            left[q, c, cell + c - 1 if c > 0 else l_edge] = 1
            right[q, c, cell + c + 1 if c < strip - 1 else r_edge] = 1
    both = np.concatenate([left, right], 0).reshape(2 * (rows + 2) * strip, -1)
    return jnp.asarray(both, BF16)


def parity_picker(frames, strip):
    half = strip // 2
    pick = np.zeros((2, frames, half, frames, strip), np.float32)
    for b in range(2):
        for t in range(frames):
            for c in range(half):
                pick[b, t, c, t, 2 * c + b] = 1
    return jnp.asarray(pick.reshape(frames * strip, frames * strip), BF16)


def encode_body(waits, *refs, links, rows, strip):
    halos, shifts, w_spatial, parity, w_temporal, w_down, refs = (*refs[:6], refs[6:])
    cells, refs = refs[:links], refs[links:]
    w_proj, refs = refs[:4], refs[4:]
    spatial, mid_out, attended_out, student_out, refs = (*refs[:4], refs[4:])
    pieces, refs = refs[:links], refs[links:]
    grid, cat, patch, top = refs
    zhi, core = place()
    frames = 2 * links
    chan = spatial.shape[-1]
    width = attended_out.shape[-1]
    tall = (rows + 2) * strip
    waits[0]()
    main = rows * strip
    for k in range(links):
        origin = lax.rem(zhi - k + links, links)
        for s in range(2):
            t = 2 * origin + (core if s == 0 else 1 - core)
            cat[: main + EDGES] = cells[k][s]
            cat[main + EDGES :] = halos[origin, s]
            moved = jnp.dot(shifts[...], cat[...], preferred_element_type=F32).astype(BF16)
            grid[:, t, :, :chan] = moved[:tall].reshape(rows + 2, strip, chan)
            grid[:, t, :, 2 * chan :] = moved[tall:].reshape(rows + 2, strip, chan)
            centre = slice(chan, 2 * chan)
            grid[0, t, :, centre] = halos[origin, s, :strip]
            grid[1 : rows + 1, t, :, centre] = cells[k][s, :main].reshape(rows, strip, chan)
            grid[rows + 1, t, :, centre] = halos[origin, s, strip : 2 * strip]
    waits[1]()
    cellcount = rows * frames * strip
    conv = jnp.dot(
        grid[:rows].reshape(cellcount, 3 * chan), w_spatial[0], preferred_element_type=F32
    )
    for d in range(1, 3):
        conv = conv + jnp.dot(
            grid[d : rows + d].reshape(cellcount, 3 * chan),
            w_spatial[d],
            preferred_element_type=F32,
        )
    conv = conv / (1.0 + jnp.exp(-conv))
    spatial[:, :2] = jnp.zeros((rows, 2, strip, chan), BF16)
    spatial[:, 2:] = conv.astype(BF16).reshape(rows, frames, strip, chan)
    for wait in waits[2:]:
        wait()
    acc = grid[1 : rows + 1, :, :, chan : 2 * chan].reshape(cellcount, chan).astype(F32)
    temporal = jnp.dot(
        spatial[:, :frames].reshape(cellcount, chan),
        w_temporal[:chan],
        preferred_element_type=F32,
    )
    for m in range(1, 3):
        temporal = temporal + jnp.dot(
            spatial[:, m : m + frames].reshape(cellcount, chan),
            w_temporal[m * chan : (m + 1) * chan],
            preferred_element_type=F32,
        )
    mid_out[...] = (acc + temporal).astype(BF16)
    line = frames * strip
    half = strip // 2
    for r in range(rows):
        both = jnp.dot(
            parity[...], mid_out[r * line : (r + 1) * line], preferred_element_type=F32
        ).astype(BF16)
        i, a = r // 2, r % 2
        span = slice(i * line // 2, (i + 1) * line // 2)
        patch[span, 2 * a * chan : (2 * a + 1) * chan] = both[: line // 2]
        patch[span, (2 * a + 1) * chan : (2 * a + 2) * chan] = both[line // 2 :]
    coarse = jnp.dot(patch[...], w_down[...], preferred_element_type=F32).astype(BF16)
    half_rows = rows // 2
    quads = (half_rows, frames, half, width)
    query = jnp.dot(coarse, w_proj[0][...], preferred_element_type=F32).astype(BF16)
    key = jnp.dot(coarse, w_proj[1][...], preferred_element_type=F32).astype(BF16)
    value = jnp.dot(coarse, w_proj[2][...], preferred_element_type=F32).astype(BF16)
    top[0] = query.astype(F32).reshape(quads)
    top[1] = key.astype(F32).reshape(quads)
    top[2] = value.astype(F32).reshape(quads)
    scale = 1.0 / math.sqrt(width)

    def attend(i, carry):
        for t in range(frames):
            q = top[0, i, t]
            scores = [
                jnp.sum(q * top[1, i, s], -1, keepdims=True) * scale for s in range(t + 1)
            ]
            best = functools.reduce(jnp.maximum, scores)
            weights = [jnp.exp(score - best) for score in scores]
            total = functools.reduce(jnp.add, weights)
            mix = functools.reduce(
                jnp.add, [weights[s] * top[2, i, s] for s in range(t + 1)]
            )
            top[3, i, t] = mix / total
        return carry

    lax.fori_loop(0, half_rows, attend, 0)
    attended = top[3].reshape(half_rows * frames * half, width).astype(BF16)
    attended_out[...] = attended
    out = jnp.dot(attended, w_proj[3][...], preferred_element_type=F32)
    student = (coarse.astype(F32) + out).astype(BF16)
    student_out[...] = student
    top[0] = student.astype(F32).reshape(quads)
    for k in range(links):
        dest = lax.rem(zhi + k, links)
        for s in range(2):
            t = 2 * dest + (core if s == 0 else 1 - core)
            pieces[k][s] = top[0, :, t].reshape(half_rows * half, width).astype(BF16)


def encode(cells, halos, w_spatial, w_temporal, w_down, w_proj, links, rows, strip):
    frames = 2 * links
    chan = w_temporal.shape[1]
    width = w_down.shape[-1]
    half = strip // 2
    points = (rows // 2) * half
    args = (
        halos,
        shift_pickers(rows, strip),
        w_spatial.reshape(3, 3 * chan, chan),
        parity_picker(frames, strip),
        w_temporal,
        w_down.reshape(4 * chan, width),
        *cells,
        *w_proj,
    )
    shapes = [
        jax.ShapeDtypeStruct((rows, frames + 2, strip, chan), BF16),
        jax.ShapeDtypeStruct((rows * frames * strip, chan), BF16),
        jax.ShapeDtypeStruct((frames * points, width), BF16),
        jax.ShapeDtypeStruct((frames * points, width), BF16),
    ] + [jax.ShapeDtypeStruct((2, points, width), BF16)] * links
    scratch = [
        pltpu.VMEM((rows + 2, frames, strip, 3 * chan), BF16),
        pltpu.VMEM((rows * strip + 2 * strip + 2 * EDGES, chan), BF16),
        pltpu.VMEM((frames * points, 4 * chan), BF16),
        pltpu.VMEM((4, rows // 2, frames, half, width), F32),
    ]
    outs = call(
        functools.partial(encode_body, links=links, rows=rows, strip=strip),
        shapes,
        args,
        scratch=scratch,
        room=32,
        manual=(1, 2, 3, 4, 5, *range(6 + links, 10 + links)),
    )
    return outs[:4], outs[4:]


def gradients_body(*refs, links, scale_mid, scale_top):
    teachers, refs = refs[:links], refs[links:]
    spatial, mid, attended, student, keep, give, t_mid, t_top, g_mid, g_top = refs
    zhi, core = place()
    rows, padded, strip, chan = spatial.shape
    frames = padded - 2
    half_rows, _, half, width = t_top.shape
    base = rows * strip
    points = half_rows * half
    for k in range(links):
        origin = lax.rem(zhi - k + links, links)
        for s in range(2):
            t = 2 * origin + (core if s == 0 else 1 - core)
            t_mid[:, t] = teachers[k][s, :base].reshape(rows, strip, chan)
            low = teachers[k][s, base : base + points].astype(F32)
            high = teachers[k][s, base + points :].astype(F32)
            t_top[:, t, :, :chan] = low.reshape(half_rows, half, chan)
            t_top[:, t, :, chan:] = high.reshape(half_rows, half, chan)
    count = rows * frames * strip
    diff = (mid[...].astype(F32) - t_mid[...].reshape(count, chan).astype(F32)).astype(BF16)
    dims = (((0,), (0,)), ((), ()))
    for m in range(3):
        g_mid[m * chan : (m + 1) * chan] = (
            lax.dot_general(
                spatial[:, m : m + frames].reshape(count, chan),
                diff,
                dims,
                preferred_element_type=F32,
            )
            * scale_mid
        )
    diff = (
        student[...].astype(F32) - t_top[...].reshape(frames * points, width)
    ).astype(BF16)
    g_top[...] = lax.dot_general(attended[...], diff, dims, preferred_element_type=F32) * scale_top
    spaces = 2 * keep.shape[0]
    n_mid = g_mid.shape[0] // (frames * spaces)
    n_top = g_top.shape[0] // (frames * spaces)
    for c in range(2):

        @pl.when(core == c)
        def _():
            for side, ref in ((c, keep), (1 - c, give)):
                for z in range(links):
                    for p in range(spaces):
                        shard = (2 * z + side) * spaces + p
                        piece = ref.at[p // 2, z, p % 2]
                        rows_mid = g_mid[shard * n_mid : (shard + 1) * n_mid]
                        rows_top = g_top[shard * n_top : (shard + 1) * n_top]
                        row = 0
                        for block in (rows_mid, rows_top):
                            for h in range(block.shape[1] // LANES):
                                part = block[:, h * LANES : (h + 1) * LANES]
                                piece[row : row + block.shape[0]] = part.astype(ref.dtype)
                                row += block.shape[0]


def gradients(teachers, spatial, mid, attended, student, links, spaces, scale_mid, scale_top):
    rows, padded, strip, chan = spatial.shape
    frames = padded - 2
    width = attended.shape[-1]
    height = (3 * chan * chan + width * width) // (frames * spaces * LANES)
    return call(
        functools.partial(
            gradients_body, links=links, scale_mid=scale_mid, scale_top=scale_top
        ),
        [
            jax.ShapeDtypeStruct((spaces // 2, links, 2, height, LANES), F32),
            jax.ShapeDtypeStruct((spaces // 2, links, 2, height, LANES), BF16),
        ],
        (*teachers, spatial, mid, attended, student),
        scratch=[
            pltpu.VMEM((rows, frames, strip, chan), BF16),
            pltpu.VMEM((rows // 2, frames, strip // 2, width), F32),
            pltpu.VMEM((3 * chan, chan), F32),
            pltpu.VMEM((width, width), F32),
        ],
        room=16,
    )


def unpack_body(*refs, links):
    mine, swapped, out = refs[:links], refs[links], refs[links + 1]
    zhi, core = place()
    half_rows, cols, width = out.shape
    half = cols // (2 * links)
    for k in range(links):
        origin = lax.rem(zhi - k + links, links)
        own = mine[k][0].astype(F32).reshape(half_rows, half, width)
        other = swapped[k].astype(F32).reshape(half_rows, half, width)
        first = jnp.where(core == 0, own, other)
        second = jnp.where(core == 0, other, own)
        begin = pl.multiple_of(origin * 2 * half, 2 * half)
        out[:, pl.ds(begin, 2 * half), :] = jnp.concatenate([first, second], 1).astype(BF16)


def finish_body(*refs):
    parts, mid, top = refs[:-2], refs[-2], refs[-1]
    total = functools.reduce(jnp.add, [part[...] for part in parts])
    row = 0
    for out in (mid, top):
        count, cols = out.shape
        for h in range(cols // LANES):
            out[:, h * LANES : (h + 1) * LANES] = total[row : row + count]
            row += count


def local(
    feats, w_spatial, w_temporal, teacher_mid, w_down, w_query, w_key, w_value, w_out, teacher_top
):
    frames = lax.axis_size("tm")
    spaces = lax.axis_size("space")
    clips = lax.axis_size("dp")
    links = frames // 2
    devices_all = clips * frames * spaces
    own = feats[0, 0]
    rows, cols, chan = own.shape
    strip = cols // frames
    half_rows, half_cols, width = teacher_top.shape[2:]
    points = half_rows * (half_cols // frames)

    def swap(block):
        return lax.ppermute(block, "tm", [(i, i ^ 1) for i in range(frames)])

    def spread(pieces):
        return [pieces[0]] + [
            lax.ppermute(pieces[k], "tm", [(i, (i + 2 * k) % frames) for i in range(frames)])
            for k in range(1, links)
        ]

    columns = [list(range(c, frames, 2)) for c in range(2)]

    def gather(pieces):
        return lax.all_to_all(pieces, "tm", 0, 0, axis_index_groups=columns, tiled=True)

    ring = [(i, (i + 1) % spaces) for i in range(spaces)]
    above = lax.ppermute(own[rows - 1], "space", ring)
    below = lax.ppermute(own[0], "space", [(j, i) for i, j in ring])
    cells = pack_main(own, swap(own), links)
    cells = spread(cells)
    other = (swap(above), swap(below))
    halo = pack_halo((above, below), other, links)
    halos = gather(halo)
    t_mid, t_top = teacher_mid[0, 0], teacher_top[0, 0]
    teachers = pack_teacher(t_mid, swap(t_mid), t_top, swap(t_top), links)
    teachers = spread(teachers)

    w_proj = (w_query, w_key, w_value, w_out)
    saved, pieces = encode(
        cells, halos, w_spatial, w_temporal, w_down, w_proj, links, rows, strip
    )
    returned = spread(pieces)
    swapped = swap(jnp.stack([piece[1] for piece in returned]))
    home = call(
        functools.partial(unpack_body, links=links),
        [jax.ShapeDtypeStruct((half_rows, half_cols, width), BF16)],
        (*returned, swapped),
    )[0]

    keep, give = gradients(
        teachers,
        *saved,
        links,
        spaces,
        1.0 / math.sqrt(rows * cols * devices_all),
        1.0 / math.sqrt(points * frames * devices_all),
    )
    part = (keep + swap(give).astype(F32)).astype(BF16)
    lines = [list(range(a, spaces, 2)) for a in range(2)]
    part = lax.all_to_all(part, "space", 0, 0, axis_index_groups=lines, tiled=True)
    part = jnp.sum(part.astype(F32), 0).astype(BF16)
    part = part.reshape(frames, *part.shape[2:])
    groups = [
        [(2 * z + c) * spaces + p + a for z in range(links) for a in range(2)]
        for c in range(2)
        for p in range(0, spaces, 2)
    ]
    part = lax.all_to_all(part, ("tm", "space"), 0, 0, axis_index_groups=groups, tiled=True)
    part = jnp.sum(part.astype(F32), 0)
    others = [
        lax.ppermute(part, "dp", [(i, (i + k) % clips) for i in range(clips)])
        for k in range(1, clips)
    ]
    n_top = width // (frames * spaces)
    grad_temporal, grad_out = call(
        finish_body,
        [
            jax.ShapeDtypeStruct((3 * chan // (frames * spaces), chan), F32),
            jax.ShapeDtypeStruct((n_top, width), F32),
        ],
        (part, *others),
    )
    return (home[None, None], grad_temporal, grad_out)


def solution(mesh):
    return jax.shard_map(
        local,
        mesh=mesh,
        in_specs=(
            P("dp", "tm", "space", None, None),
            P(),
            P(),
            P("dp", "tm", "space", None, None),
            P(),
            P(),
            P(),
            P(),
            P(),
            P("dp", "tm", "space", None, None),
        ),
        out_specs=(
            P("dp", "tm", "space", None, None),
            P(("tm", "space"), None),
            P(("tm", "space"), None),
        ),
        check_vma=False,
    )
```

```python
import functools
import math

import jax
import jax.numpy as jnp
import numpy as np
from jax import lax
from jax.experimental import pallas as pl
from jax.experimental.pallas import tpu as pltpu
from jax.sharding import PartitionSpec as P


F32 = jnp.float32
BF16 = jnp.bfloat16
LANES = 128


def call(body, out_shape, args, scratch=(), room=8, manual=()):
    specs = [
        pl.BlockSpec(memory_space=pltpu.HBM if i in manual else pltpu.VMEM)
        for i in range(len(args))
    ]
    outs = [pl.BlockSpec(memory_space=pltpu.VMEM) for _ in out_shape]
    held = [pltpu.VMEM(args[i].shape, args[i].dtype) for i in manual]

    def run(*refs):
        ins, rest = list(refs[: len(args)]), refs[len(args) :]
        waits = []
        if manual:
            rest, local_refs, sems = rest[: -len(manual) - 1], rest[-len(manual) - 1 : -1], rest[-1]
            for n, i in enumerate(manual):
                copy = pltpu.make_async_copy(ins[i], local_refs[n], sems.at[n])
                copy.start()
                waits.append(copy.wait)
                ins[i] = local_refs[n]
            body(waits, *ins, *rest)
        else:
            body(*ins, *rest)

    extra = held + [pltpu.SemaphoreType.DMA((len(manual),))] if manual else []
    return pl.pallas_call(
        run,
        out_shape=out_shape,
        in_specs=specs,
        out_specs=outs,
        scratch_shapes=[*scratch, *extra],
        compiler_params=pltpu.CompilerParams(vmem_limit_bytes=room << 20),
    )(
        *[
            pltpu.with_memory_space_constraint(arg, pltpu.HBM) if i in manual else arg
            for i, arg in enumerate(args)
        ]
    )


def place():
    index = lax.axis_index("tm")
    return index // 2, index % 2


EDGES = 16
CORNERS = 8


def edge_picker(count, cols, strip, height):
    strips = cols // strip
    pick = np.zeros((strips, height, count * cols), np.float32)
    for j in range(strips):
        for r in range(count):
            if j > 0:
                pick[j, r, r * cols + j * strip - 1] = 1
            if j < strips - 1:
                pick[j, count + r, r * cols + (j + 1) * strip] = 1
    return jnp.asarray(pick.reshape(strips * height, count * cols), BF16)


def pack_piece(tall, edges, out, s, j):
    count, cols, chan = tall.shape
    strip = cols // edges.shape[0]
    begin = pl.multiple_of(j * strip, strip)
    out[s, : count * strip] = tall[:, pl.ds(begin, strip), :].reshape(count * strip, chan)
    out[s, count * strip :] = edges[j]


def find_edges(tall, pick, edges):
    count, cols, chan = tall.shape
    flat = tall[...].reshape(count * cols, chan)
    found = jnp.dot(pick, flat, preferred_element_type=F32).astype(BF16)
    edges[...] = found.reshape(edges.shape)


def pack_main_body(waits, own, partner, pick, *refs, links):
    outs, edges = refs[:links], refs[links]
    zhi, core = place()
    for wait in waits:
        wait()
    for s, source in enumerate((own, partner)):
        find_edges(source, pick[...], edges)
        for k in range(links):
            pack_piece(source, edges, outs[k], s, 2 * lax.rem(zhi + k, links) + core)


def pack_main(own, partner, links):
    rows, cols, chan = own.shape
    strip = cols // (2 * links)
    return call(
        functools.partial(pack_main_body, links=links),
        [jax.ShapeDtypeStruct((2, rows * strip + EDGES, chan), BF16)] * links,
        (own, partner, edge_picker(rows, cols, strip, EDGES)),
        scratch=[pltpu.VMEM((2 * links, EDGES, chan), BF16)],
        manual=(0, 2),
    )


def pack_halo_body(*refs, links):
    sources, out = (refs[:2], refs[2:4]), refs[4]
    tall, edges = refs[5:]
    _, core = place()
    count, cols, _ = tall.shape
    strip = cols // (2 * links)
    shape = (2 * links * CORNERS, count * cols)
    line = lax.broadcasted_iota(jnp.int32, shape, 0)
    spot = lax.broadcasted_iota(jnp.int32, shape, 1)
    j, q = line // CORNERS, line % CORNERS
    left = (q < count) & (j > 0) & (spot == q * cols + j * strip - 1)
    right = (q >= count) & (q < 2 * count) & (j < 2 * links - 1)
    right = right & (spot == (q - count) * cols + (j + 1) * strip)
    pick = jnp.where(left | right, 1.0, 0.0).astype(BF16)
    index = lax.axis_index("space")
    first, last = index == 0, index == lax.axis_size("space") - 1
    for s, (above, below) in enumerate(sources):
        tall[0] = jnp.where(first, jnp.zeros_like(above), above[...])
        tall[1] = jnp.where(last, jnp.zeros_like(below), below[...])
        find_edges(tall, pick, edges)
        for k in range(links):
            pack_piece(tall, edges, out.at[k], s, 2 * k + core)


def pack_halo(own, partner, links):
    cols, chan = own[0].shape
    strip = cols // (2 * links)
    return call(
        functools.partial(pack_halo_body, links=links),
        [jax.ShapeDtypeStruct((links, 2, 2 * strip + CORNERS, chan), BF16)],
        (*own, *partner),
        scratch=[
            pltpu.VMEM((2, cols, chan), BF16),
            pltpu.VMEM((2 * links, CORNERS, chan), BF16),
        ],
    )[0]


def pack_teacher_body(waits, own_mid, partner_mid, own_top, partner_top, *outs, links):
    zhi, core = place()
    for wait in waits:
        wait()
    rows, cols, chan = own_mid.shape
    half_rows, half_cols, width = own_top.shape
    strip = cols // (2 * links)
    half = half_cols // (2 * links)
    base = rows * strip
    points = half_rows * half
    for k in range(links):
        dest = lax.rem(zhi + k, links)
        j = 2 * dest + core
        for s, (mid, top) in enumerate(((own_mid, own_top), (partner_mid, partner_top))):
            begin = pl.multiple_of(j * strip, strip)
            outs[k][s, :base] = mid[:, pl.ds(begin, strip), :].reshape(base, chan)
            begin = pl.multiple_of(dest * 2 * half, 2 * half)
            both = top[:, pl.ds(begin, 2 * half), :].astype(F32)
            mine = jnp.where(core == 0, both[:, :half], both[:, half:])
            mine = mine.reshape(points, width)
            outs[k][s, base : base + points] = mine[:, :chan].astype(BF16)
            outs[k][s, base + points :] = mine[:, chan:].astype(BF16)


def pack_teacher(own_mid, partner_mid, own_top, partner_top, links):
    rows, cols, chan = own_mid.shape
    half_rows, half_cols, width = own_top.shape
    points = half_rows * (half_cols // (2 * links))
    height = rows * (cols // (2 * links)) + points * (width // chan)
    return call(
        functools.partial(pack_teacher_body, links=links),
        [jax.ShapeDtypeStruct((2, height, chan), BF16)] * links,
        (own_mid, partner_mid, own_top, partner_top),
        manual=(0, 2),
    )


def shift_pickers(rows, strip):
    main = rows * strip
    halo = main + EDGES
    corner = halo + 2 * strip
    left = np.zeros((rows + 2, strip, corner + CORNERS), np.float32)
    right = np.zeros_like(left)
    for q in range(rows + 2):
        if q == 0:
            cell, l_edge, r_edge = halo, corner, corner + 2
        elif q == rows + 1:
            cell, l_edge, r_edge = halo + strip, corner + 1, corner + 3
        else:
            cell, l_edge, r_edge = (q - 1) * strip, main + q - 1, main + rows + q - 1
        for c in range(strip):
            left[q, c, cell + c - 1 if c > 0 else l_edge] = 1
            right[q, c, cell + c + 1 if c < strip - 1 else r_edge] = 1
    both = np.concatenate([left, right], 0).reshape(2 * (rows + 2) * strip, -1)
    return jnp.asarray(both, BF16)


def parity_picker(frames, strip):
    half = strip // 2
    pick = np.zeros((2, frames, half, frames, strip), np.float32)
    for b in range(2):
        for t in range(frames):
            for c in range(half):
                pick[b, t, c, t, 2 * c + b] = 1
    return jnp.asarray(pick.reshape(frames * strip, frames * strip), BF16)


def encode_body(waits, *refs, links, rows, strip):
    halos, shifts, w_spatial, parity, w_temporal, w_down, refs = (*refs[:6], refs[6:])
    cells, refs = refs[:links], refs[links:]
    w_proj, refs = refs[:4], refs[4:]
    spatial, mid_out, attended_out, student_out, refs = (*refs[:4], refs[4:])
    pieces, refs = refs[:links], refs[links:]
    grid, cat, patch, top = refs
    zhi, core = place()
    frames = 2 * links
    chan = spatial.shape[-1]
    width = attended_out.shape[-1]
    tall = (rows + 2) * strip
    waits[0]()
    main = rows * strip
    for k in range(links):
        origin = lax.rem(zhi - k + links, links)
        for s in range(2):
            t = 2 * origin + (core if s == 0 else 1 - core)
            cat[: main + EDGES] = cells[k][s]
            cat[main + EDGES :] = halos[origin, s]
            moved = jnp.dot(shifts[...], cat[...], preferred_element_type=F32).astype(BF16)
            grid[:, t, :, :chan] = moved[:tall].reshape(rows + 2, strip, chan)
            grid[:, t, :, 2 * chan :] = moved[tall:].reshape(rows + 2, strip, chan)
            centre = slice(chan, 2 * chan)
            grid[0, t, :, centre] = halos[origin, s, :strip]
            grid[1 : rows + 1, t, :, centre] = cells[k][s, :main].reshape(rows, strip, chan)
            grid[rows + 1, t, :, centre] = halos[origin, s, strip : 2 * strip]
    waits[1]()
    cellcount = rows * frames * strip
    conv = jnp.dot(
        grid[:rows].reshape(cellcount, 3 * chan), w_spatial[0], preferred_element_type=F32
    )
    for d in range(1, 3):
        conv = conv + jnp.dot(
            grid[d : rows + d].reshape(cellcount, 3 * chan),
            w_spatial[d],
            preferred_element_type=F32,
        )
    conv = conv / (1.0 + jnp.exp(-conv))
    spatial[:, :2] = jnp.zeros((rows, 2, strip, chan), BF16)
    spatial[:, 2:] = conv.astype(BF16).reshape(rows, frames, strip, chan)
    for wait in waits[2:]:
        wait()
    acc = grid[1 : rows + 1, :, :, chan : 2 * chan].reshape(cellcount, chan).astype(F32)
    temporal = jnp.dot(
        spatial[:, :frames].reshape(cellcount, chan),
        w_temporal[:chan],
        preferred_element_type=F32,
    )
    for m in range(1, 3):
        temporal = temporal + jnp.dot(
            spatial[:, m : m + frames].reshape(cellcount, chan),
            w_temporal[m * chan : (m + 1) * chan],
            preferred_element_type=F32,
        )
    mid_out[...] = (acc + temporal).astype(BF16)
    line = frames * strip
    half = strip // 2
    for r in range(rows):
        both = jnp.dot(
            parity[...], mid_out[r * line : (r + 1) * line], preferred_element_type=F32
        ).astype(BF16)
        i, a = r // 2, r % 2
        span = slice(i * line // 2, (i + 1) * line // 2)
        patch[span, 2 * a * chan : (2 * a + 1) * chan] = both[: line // 2]
        patch[span, (2 * a + 1) * chan : (2 * a + 2) * chan] = both[line // 2 :]
    coarse = jnp.dot(patch[...], w_down[...], preferred_element_type=F32).astype(BF16)
    half_rows = rows // 2
    quads = (half_rows, frames, half, width)
    query = jnp.dot(coarse, w_proj[0][...], preferred_element_type=F32).astype(BF16)
    key = jnp.dot(coarse, w_proj[1][...], preferred_element_type=F32).astype(BF16)
    value = jnp.dot(coarse, w_proj[2][...], preferred_element_type=F32).astype(BF16)
    top[0] = query.astype(F32).reshape(quads)
    top[1] = key.astype(F32).reshape(quads)
    top[2] = value.astype(F32).reshape(quads)
    scale = 1.0 / math.sqrt(width)

    def attend(i, carry):
        for t in range(frames):
            q = top[0, i, t]
            scores = [
                jnp.sum(q * top[1, i, s], -1, keepdims=True) * scale for s in range(t + 1)
            ]
            best = functools.reduce(jnp.maximum, scores)
            weights = [jnp.exp(score - best) for score in scores]
            total = functools.reduce(jnp.add, weights)
            mix = functools.reduce(
                jnp.add, [weights[s] * top[2, i, s] for s in range(t + 1)]
            )
            top[3, i, t] = mix / total
        return carry

    lax.fori_loop(0, half_rows, attend, 0)
    attended = top[3].reshape(half_rows * frames * half, width).astype(BF16)
    attended_out[...] = attended
    out = jnp.dot(attended, w_proj[3][...], preferred_element_type=F32)
    student = (coarse.astype(F32) + out).astype(BF16)
    student_out[...] = student
    top[0] = student.astype(F32).reshape(quads)
    for k in range(links):
        dest = lax.rem(zhi + k, links)
        for s in range(2):
            t = 2 * dest + (core if s == 0 else 1 - core)
            pieces[k][s] = top[0, :, t].reshape(half_rows * half, width).astype(BF16)


def encode(cells, halos, w_spatial, w_temporal, w_down, w_proj, links, rows, strip):
    frames = 2 * links
    chan = w_temporal.shape[1]
    width = w_down.shape[-1]
    half = strip // 2
    points = (rows // 2) * half
    args = (
        halos,
        shift_pickers(rows, strip),
        w_spatial.reshape(3, 3 * chan, chan),
        parity_picker(frames, strip),
        w_temporal,
        w_down.reshape(4 * chan, width),
        *cells,
        *w_proj,
    )
    shapes = [
        jax.ShapeDtypeStruct((rows, frames + 2, strip, chan), BF16),
        jax.ShapeDtypeStruct((rows * frames * strip, chan), BF16),
        jax.ShapeDtypeStruct((frames * points, width), BF16),
        jax.ShapeDtypeStruct((frames * points, width), BF16),
    ] + [jax.ShapeDtypeStruct((2, points, width), BF16)] * links
    scratch = [
        pltpu.VMEM((rows + 2, frames, strip, 3 * chan), BF16),
        pltpu.VMEM((rows * strip + EDGES + 2 * strip + CORNERS, chan), BF16),
        pltpu.VMEM((frames * points, 4 * chan), BF16),
        pltpu.VMEM((4, rows // 2, frames, half, width), F32),
    ]
    outs = call(
        functools.partial(encode_body, links=links, rows=rows, strip=strip),
        shapes,
        args,
        scratch=scratch,
        room=32,
        manual=(1, 2, 3, 4, 5, *range(6 + links, 10 + links)),
    )
    return outs[:4], outs[4:]


def gradients_body(*refs, links, scale_mid, scale_top):
    teachers, refs = refs[:links], refs[links:]
    spatial, mid, attended, student, keep, give, t_mid, t_top, g_mid, g_top = refs
    zhi, core = place()
    rows, padded, strip, chan = spatial.shape
    frames = padded - 2
    half_rows, _, half, width = t_top.shape
    base = rows * strip
    points = half_rows * half
    for k in range(links):
        origin = lax.rem(zhi - k + links, links)
        for s in range(2):
            t = 2 * origin + (core if s == 0 else 1 - core)
            t_mid[:, t] = teachers[k][s, :base].reshape(rows, strip, chan)
            low = teachers[k][s, base : base + points].astype(F32)
            high = teachers[k][s, base + points :].astype(F32)
            t_top[:, t, :, :chan] = low.reshape(half_rows, half, chan)
            t_top[:, t, :, chan:] = high.reshape(half_rows, half, chan)
    count = rows * frames * strip
    diff = (mid[...].astype(F32) - t_mid[...].reshape(count, chan).astype(F32)).astype(BF16)
    dims = (((0,), (0,)), ((), ()))
    for m in range(3):
        g_mid[m * chan : (m + 1) * chan] = (
            lax.dot_general(
                spatial[:, m : m + frames].reshape(count, chan),
                diff,
                dims,
                preferred_element_type=F32,
            )
            * scale_mid
        )
    diff = (
        student[...].astype(F32) - t_top[...].reshape(frames * points, width)
    ).astype(BF16)
    g_top[...] = lax.dot_general(attended[...], diff, dims, preferred_element_type=F32) * scale_top
    spaces = 2 * keep.shape[0]
    n_mid = g_mid.shape[0] // (frames * spaces)
    n_top = g_top.shape[0] // (frames * spaces)
    for c in range(2):

        @pl.when(core == c)
        def _():
            for side, ref in ((c, keep), (1 - c, give)):
                for z in range(links):
                    for p in range(spaces):
                        shard = (2 * z + side) * spaces + p
                        piece = ref.at[p // 2, z, p % 2]
                        rows_mid = g_mid[shard * n_mid : (shard + 1) * n_mid]
                        rows_top = g_top[shard * n_top : (shard + 1) * n_top]
                        row = 0
                        for block in (rows_mid, rows_top):
                            for h in range(block.shape[1] // LANES):
                                part = block[:, h * LANES : (h + 1) * LANES]
                                piece[row : row + block.shape[0]] = part.astype(ref.dtype)
                                row += block.shape[0]


def gradients(teachers, spatial, mid, attended, student, links, spaces, scale_mid, scale_top):
    rows, padded, strip, chan = spatial.shape
    frames = padded - 2
    width = attended.shape[-1]
    height = (3 * chan * chan + width * width) // (frames * spaces * LANES)
    return call(
        functools.partial(
            gradients_body, links=links, scale_mid=scale_mid, scale_top=scale_top
        ),
        [
            jax.ShapeDtypeStruct((spaces // 2, links, 2, height, LANES), F32),
            jax.ShapeDtypeStruct((spaces // 2, links, 2, height, LANES), BF16),
        ],
        (*teachers, spatial, mid, attended, student),
        scratch=[
            pltpu.VMEM((rows, frames, strip, chan), BF16),
            pltpu.VMEM((rows // 2, frames, strip // 2, width), F32),
            pltpu.VMEM((3 * chan, chan), F32),
            pltpu.VMEM((width, width), F32),
        ],
        room=16,
    )


def unpack_body(*refs, links):
    mine, swapped, out = refs[:links], refs[links], refs[links + 1]
    zhi, core = place()
    half_rows, cols, width = out.shape
    half = cols // (2 * links)
    for k in range(links):
        origin = lax.rem(zhi - k + links, links)
        own = mine[k][0].astype(F32).reshape(half_rows, half, width)
        other = swapped[k].astype(F32).reshape(half_rows, half, width)
        first = jnp.where(core == 0, own, other)
        second = jnp.where(core == 0, other, own)
        begin = pl.multiple_of(origin * 2 * half, 2 * half)
        out[:, pl.ds(begin, 2 * half), :] = jnp.concatenate([first, second], 1).astype(BF16)


def finish_body(*refs):
    parts, mid, top = refs[:-2], refs[-2], refs[-1]
    total = functools.reduce(jnp.add, [part[...] for part in parts])
    row = 0
    for out in (mid, top):
        count, cols = out.shape
        for h in range(cols // LANES):
            out[:, h * LANES : (h + 1) * LANES] = total[row : row + count]
            row += count


def local(
    feats, w_spatial, w_temporal, teacher_mid, w_down, w_query, w_key, w_value, w_out, teacher_top
):
    frames = lax.axis_size("tm")
    spaces = lax.axis_size("space")
    clips = lax.axis_size("dp")
    links = frames // 2
    devices_all = clips * frames * spaces
    own = feats[0, 0]
    rows, cols, chan = own.shape
    strip = cols // frames
    half_rows, half_cols, width = teacher_top.shape[2:]
    points = half_rows * (half_cols // frames)

    def swap(block):
        return lax.ppermute(block, "tm", [(i, i ^ 1) for i in range(frames)])

    def spread(pieces):
        return [pieces[0]] + [
            lax.ppermute(pieces[k], "tm", [(i, (i + 2 * k) % frames) for i in range(frames)])
            for k in range(1, links)
        ]

    columns = [list(range(c, frames, 2)) for c in range(2)]

    def gather(pieces):
        return lax.all_to_all(pieces, "tm", 0, 0, axis_index_groups=columns, tiled=True)

    ring = [(i, (i + 1) % spaces) for i in range(spaces)]
    above = lax.ppermute(own[rows - 1], "space", ring)
    below = lax.ppermute(own[0], "space", [(j, i) for i, j in ring])
    cells = pack_main(own, swap(own), links)
    cells = spread(cells)
    other = (swap(above), swap(below))
    halo = pack_halo((above, below), other, links)
    halos = gather(halo)
    t_mid, t_top = teacher_mid[0, 0], teacher_top[0, 0]
    teachers = pack_teacher(t_mid, swap(t_mid), t_top, swap(t_top), links)
    teachers = spread(teachers)

    w_proj = (w_query, w_key, w_value, w_out)
    saved, pieces = encode(
        cells, halos, w_spatial, w_temporal, w_down, w_proj, links, rows, strip
    )
    returned = spread(pieces)
    swapped = swap(jnp.stack([piece[1] for piece in returned]))
    home = call(
        functools.partial(unpack_body, links=links),
        [jax.ShapeDtypeStruct((half_rows, half_cols, width), BF16)],
        (*returned, swapped),
    )[0]

    keep, give = gradients(
        teachers,
        *saved,
        links,
        spaces,
        1.0 / math.sqrt(rows * cols * devices_all),
        1.0 / math.sqrt(points * frames * devices_all),
    )
    part = (keep + swap(give).astype(F32)).astype(BF16)
    lines = [list(range(a, spaces, 2)) for a in range(2)]
    part = lax.all_to_all(part, "space", 0, 0, axis_index_groups=lines, tiled=True)
    part = jnp.sum(part.astype(F32), 0).astype(BF16)
    part = part.reshape(frames, *part.shape[2:])
    groups = [
        [(2 * z + c) * spaces + p + a for z in range(links) for a in range(2)]
        for c in range(2)
        for p in range(0, spaces, 2)
    ]
    part = lax.all_to_all(part, ("tm", "space"), 0, 0, axis_index_groups=groups, tiled=True)
    part = jnp.sum(part.astype(F32), 0)
    others = [lax.ppermute(part, "dp", [(i, i ^ k) for i in range(clips)]) for k in range(1, clips)]
    n_top = width // (frames * spaces)
    grad_temporal, grad_out = call(
        finish_body,
        [
            jax.ShapeDtypeStruct((3 * chan // (frames * spaces), chan), F32),
            jax.ShapeDtypeStruct((n_top, width), F32),
        ],
        (part, *others),
    )
    return (home[None, None], grad_temporal, grad_out)


def solution(mesh):
    return jax.shard_map(
        local,
        mesh=mesh,
        in_specs=(
            P("dp", "tm", "space", None, None),
            P(),
            P(),
            P("dp", "tm", "space", None, None),
            P(),
            P(),
            P(),
            P(),
            P(),
            P("dp", "tm", "space", None, None),
        ),
        out_specs=(
            P("dp", "tm", "space", None, None),
            P(("tm", "space"), None),
            P(("tm", "space"), None),
        ),
        check_vma=False,
    )
```

```python
import functools
import math

import jax
import jax.numpy as jnp
import numpy as np
from jax import lax
from jax.experimental import pallas as pl
from jax.experimental.pallas import tpu as pltpu
from jax.sharding import PartitionSpec as P


F32 = jnp.float32
BF16 = jnp.bfloat16
LANES = 128


def call(body, out_shape, args, scratch=(), room=8, manual=()):
    specs = [
        pl.BlockSpec(memory_space=pltpu.HBM if i in manual else pltpu.VMEM)
        for i in range(len(args))
    ]
    outs = [pl.BlockSpec(memory_space=pltpu.VMEM) for _ in out_shape]
    held = [pltpu.VMEM(args[i].shape, args[i].dtype) for i in manual]

    def run(*refs):
        ins, rest = list(refs[: len(args)]), refs[len(args) :]
        waits = []
        if manual:
            rest, local_refs, sems = rest[: -len(manual) - 1], rest[-len(manual) - 1 : -1], rest[-1]
            for n, i in enumerate(manual):
                copy = pltpu.make_async_copy(ins[i], local_refs[n], sems.at[n])
                copy.start()
                waits.append(copy.wait)
                ins[i] = local_refs[n]
            body(waits, *ins, *rest)
        else:
            body(*ins, *rest)

    extra = held + [pltpu.SemaphoreType.DMA((len(manual),))] if manual else []
    return pl.pallas_call(
        run,
        out_shape=out_shape,
        in_specs=specs,
        out_specs=outs,
        scratch_shapes=[*scratch, *extra],
        compiler_params=pltpu.CompilerParams(vmem_limit_bytes=room << 20),
    )(
        *[
            pltpu.with_memory_space_constraint(arg, pltpu.HBM) if i in manual else arg
            for i, arg in enumerate(args)
        ]
    )


def place():
    index = lax.axis_index("tm")
    return index // 2, index % 2


EDGES = 16
CORNERS = 8


def pack_piece(tall, edges, out, s, j):
    count, cols, chan = tall.shape
    strip = cols // edges.shape[0]
    begin = pl.multiple_of(j * strip, strip)
    out[s, : count * strip] = tall[:, pl.ds(begin, strip), :].reshape(count * strip, chan)
    out[s, count * strip :] = edges[j]


def make_picker(count, cols, strips, height):
    strip = cols // strips
    shape = (strips * height, count * cols)
    line = lax.broadcasted_iota(jnp.int32, shape, 0)
    spot = lax.broadcasted_iota(jnp.int32, shape, 1)
    j, q = line // height, line % height
    left = (q < count) & (j > 0) & (spot == q * cols + j * strip - 1)
    right = (q >= count) & (q < 2 * count) & (j < strips - 1)
    right = right & (spot == (q - count) * cols + (j + 1) * strip)
    return jnp.where(left | right, 1.0, 0.0).astype(BF16)


def find_edges(tall, pick, edges):
    count, cols, chan = tall.shape
    flat = tall[...].reshape(count * cols, chan)
    found = jnp.dot(pick, flat, preferred_element_type=F32).astype(BF16)
    edges[...] = found.reshape(edges.shape)


def pack_main_body(waits, own, partner, *refs, links):
    outs, edges = refs[:links], refs[links]
    zhi, core = place()
    count, cols, _ = own.shape
    pick = make_picker(count, cols, 2 * links, EDGES)
    for s, source in ((1, partner), (0, own)):
        if s == 0:
            for wait in waits:
                wait()
        find_edges(source, pick, edges)
        for k in range(links):
            pack_piece(source, edges, outs[k], s, 2 * lax.rem(zhi + k, links) + core)


def pack_main(own, partner, links):
    rows, cols, chan = own.shape
    strip = cols // (2 * links)
    return call(
        functools.partial(pack_main_body, links=links),
        [jax.ShapeDtypeStruct((2, rows * strip + EDGES, chan), BF16)] * links,
        (own, partner),
        scratch=[pltpu.VMEM((2 * links, EDGES, chan), BF16)],
        manual=(0,),
    )


def pack_halo_body(*refs, links):
    sources, out = (refs[:2], refs[2:4]), refs[4]
    tall, edges = refs[5:]
    _, core = place()
    count, cols, _ = tall.shape
    pick = make_picker(count, cols, 2 * links, CORNERS)
    index = lax.axis_index("space")
    first, last = index == 0, index == lax.axis_size("space") - 1
    for s, (above, below) in enumerate(sources):
        tall[0] = jnp.where(first, jnp.zeros_like(above), above[...])
        tall[1] = jnp.where(last, jnp.zeros_like(below), below[...])
        find_edges(tall, pick, edges)
        for k in range(links):
            pack_piece(tall, edges, out.at[k], s, 2 * k + core)


def pack_halo(own, partner, links):
    cols, chan = own[0].shape
    strip = cols // (2 * links)
    return call(
        functools.partial(pack_halo_body, links=links),
        [jax.ShapeDtypeStruct((links, 2, 2 * strip + CORNERS, chan), BF16)],
        (*own, *partner),
        scratch=[
            pltpu.VMEM((2, cols, chan), BF16),
            pltpu.VMEM((2 * links, CORNERS, chan), BF16),
        ],
    )[0]


def pack_teacher_body(waits, own_mid, partner_mid, own_top, partner_top, *outs, links):
    zhi, core = place()
    rows, cols, chan = own_mid.shape
    half_rows, half_cols, width = own_top.shape
    strip = cols // (2 * links)
    half = half_cols // (2 * links)
    base = rows * strip
    points = half_rows * half
    for s, mid, top in ((1, partner_mid, partner_top), (0, own_mid, own_top)):
        if s == 0:
            for wait in waits:
                wait()
        for k in range(links):
            dest = lax.rem(zhi + k, links)
            j = 2 * dest + core
            begin = pl.multiple_of(j * strip, strip)
            outs[k][s, :base] = mid[:, pl.ds(begin, strip), :].reshape(base, chan)
            begin = pl.multiple_of(dest * 2 * half, 2 * half)
            both = top[:, pl.ds(begin, 2 * half), :].astype(F32)
            mine = jnp.where(core == 0, both[:, :half], both[:, half:])
            mine = mine.reshape(points, width)
            outs[k][s, base : base + points] = mine[:, :chan].astype(BF16)
            outs[k][s, base + points :] = mine[:, chan:].astype(BF16)


def pack_teacher(own_mid, partner_mid, own_top, partner_top, links):
    rows, cols, chan = own_mid.shape
    half_rows, half_cols, width = own_top.shape
    points = half_rows * (half_cols // (2 * links))
    height = rows * (cols // (2 * links)) + points * (width // chan)
    return call(
        functools.partial(pack_teacher_body, links=links),
        [jax.ShapeDtypeStruct((2, height, chan), BF16)] * links,
        (own_mid, partner_mid, own_top, partner_top),
        manual=(0, 2),
    )


def shift_pickers(rows, strip):
    main = rows * strip
    halo = main + EDGES
    corner = halo + 2 * strip
    left = np.zeros((rows + 2, strip, corner + CORNERS), np.float32)
    right = np.zeros_like(left)
    for q in range(rows + 2):
        if q == 0:
            cell, l_edge, r_edge = halo, corner, corner + 2
        elif q == rows + 1:
            cell, l_edge, r_edge = halo + strip, corner + 1, corner + 3
        else:
            cell, l_edge, r_edge = (q - 1) * strip, main + q - 1, main + rows + q - 1
        for c in range(strip):
            left[q, c, cell + c - 1 if c > 0 else l_edge] = 1
            right[q, c, cell + c + 1 if c < strip - 1 else r_edge] = 1
    both = np.concatenate([left, right], 0).reshape(2 * (rows + 2) * strip, -1)
    return jnp.asarray(both, BF16)


def parity_picker(frames, strip):
    half = strip // 2
    pick = np.zeros((2, frames, half, frames, strip), np.float32)
    for b in range(2):
        for t in range(frames):
            for c in range(half):
                pick[b, t, c, t, 2 * c + b] = 1
    return jnp.asarray(pick.reshape(frames * strip, frames * strip), BF16)


def encode_body(waits, *refs, links, rows, strip):
    halos, shifts, w_spatial, parity, w_temporal, w_down, refs = (*refs[:6], refs[6:])
    cells, refs = refs[:links], refs[links:]
    w_proj, refs = refs[:4], refs[4:]
    spatial, mid_out, attended_out, student_out, refs = (*refs[:4], refs[4:])
    pieces, refs = refs[:links], refs[links:]
    grid, cat, patch, top = refs
    zhi, core = place()
    frames = 2 * links
    chan = spatial.shape[-1]
    width = attended_out.shape[-1]
    tall = (rows + 2) * strip
    waits[0]()
    main = rows * strip
    for k in range(links):
        origin = lax.rem(zhi - k + links, links)
        for s in range(2):
            t = 2 * origin + (core if s == 0 else 1 - core)
            cat[: main + EDGES] = cells[k][s]
            cat[main + EDGES :] = halos[origin, s]
            moved = jnp.dot(shifts[...], cat[...], preferred_element_type=F32).astype(BF16)
            grid[:, t, :, :chan] = moved[:tall].reshape(rows + 2, strip, chan)
            grid[:, t, :, 2 * chan :] = moved[tall:].reshape(rows + 2, strip, chan)
            centre = slice(chan, 2 * chan)
            grid[0, t, :, centre] = halos[origin, s, :strip]
            grid[1 : rows + 1, t, :, centre] = cells[k][s, :main].reshape(rows, strip, chan)
            grid[rows + 1, t, :, centre] = halos[origin, s, strip : 2 * strip]
    waits[1]()
    cellcount = rows * frames * strip
    conv = jnp.dot(
        grid[:rows].reshape(cellcount, 3 * chan), w_spatial[0], preferred_element_type=F32
    )
    for d in range(1, 3):
        conv = conv + jnp.dot(
            grid[d : rows + d].reshape(cellcount, 3 * chan),
            w_spatial[d],
            preferred_element_type=F32,
        )
    conv = conv / (1.0 + jnp.exp(-conv))
    spatial[:, :2] = jnp.zeros((rows, 2, strip, chan), BF16)
    spatial[:, 2:] = conv.astype(BF16).reshape(rows, frames, strip, chan)
    for wait in waits[2:]:
        wait()
    acc = grid[1 : rows + 1, :, :, chan : 2 * chan].reshape(cellcount, chan).astype(F32)
    temporal = jnp.dot(
        spatial[:, :frames].reshape(cellcount, chan),
        w_temporal[:chan],
        preferred_element_type=F32,
    )
    for m in range(1, 3):
        temporal = temporal + jnp.dot(
            spatial[:, m : m + frames].reshape(cellcount, chan),
            w_temporal[m * chan : (m + 1) * chan],
            preferred_element_type=F32,
        )
    mid_out[...] = (acc + temporal).astype(BF16)
    line = frames * strip
    half = strip // 2
    for r in range(rows):
        both = jnp.dot(
            parity[...], mid_out[r * line : (r + 1) * line], preferred_element_type=F32
        ).astype(BF16)
        i, a = r // 2, r % 2
        span = slice(i * line // 2, (i + 1) * line // 2)
        patch[span, 2 * a * chan : (2 * a + 1) * chan] = both[: line // 2]
        patch[span, (2 * a + 1) * chan : (2 * a + 2) * chan] = both[line // 2 :]
    coarse = jnp.dot(patch[...], w_down[...], preferred_element_type=F32).astype(BF16)
    half_rows = rows // 2
    quads = (half_rows, frames, half, width)
    query = jnp.dot(coarse, w_proj[0][...], preferred_element_type=F32).astype(BF16)
    key = jnp.dot(coarse, w_proj[1][...], preferred_element_type=F32).astype(BF16)
    value = jnp.dot(coarse, w_proj[2][...], preferred_element_type=F32).astype(BF16)
    top[0] = query.astype(F32).reshape(quads)
    top[1] = key.astype(F32).reshape(quads)
    top[2] = value.astype(F32).reshape(quads)
    scale = 1.0 / math.sqrt(width)

    def attend(i, carry):
        for t in range(frames):
            q = top[0, i, t]
            scores = [
                jnp.sum(q * top[1, i, s], -1, keepdims=True) * scale for s in range(t + 1)
            ]
            best = functools.reduce(jnp.maximum, scores)
            weights = [jnp.exp(score - best) for score in scores]
            total = functools.reduce(jnp.add, weights)
            mix = functools.reduce(
                jnp.add, [weights[s] * top[2, i, s] for s in range(t + 1)]
            )
            top[3, i, t] = mix / total
        return carry

    lax.fori_loop(0, half_rows, attend, 0)
    attended = top[3].reshape(half_rows * frames * half, width).astype(BF16)
    attended_out[...] = attended
    out = jnp.dot(attended, w_proj[3][...], preferred_element_type=F32)
    student = (coarse.astype(F32) + out).astype(BF16)
    student_out[...] = student
    top[0] = student.astype(F32).reshape(quads)
    for k in range(links):
        dest = lax.rem(zhi + k, links)
        for s in range(2):
            t = 2 * dest + (core if s == 0 else 1 - core)
            pieces[k][s] = top[0, :, t].reshape(half_rows * half, width).astype(BF16)


def encode(cells, halos, w_spatial, w_temporal, w_down, w_proj, links, rows, strip):
    frames = 2 * links
    chan = w_temporal.shape[1]
    width = w_down.shape[-1]
    half = strip // 2
    points = (rows // 2) * half
    args = (
        halos,
        shift_pickers(rows, strip),
        w_spatial.reshape(3, 3 * chan, chan),
        parity_picker(frames, strip),
        w_temporal,
        w_down.reshape(4 * chan, width),
        *cells,
        *w_proj,
    )
    shapes = [
        jax.ShapeDtypeStruct((rows, frames + 2, strip, chan), BF16),
        jax.ShapeDtypeStruct((rows * frames * strip, chan), BF16),
        jax.ShapeDtypeStruct((frames * points, width), BF16),
        jax.ShapeDtypeStruct((frames * points, width), BF16),
    ] + [jax.ShapeDtypeStruct((2, points, width), BF16)] * links
    scratch = [
        pltpu.VMEM((rows + 2, frames, strip, 3 * chan), BF16),
        pltpu.VMEM((rows * strip + EDGES + 2 * strip + CORNERS, chan), BF16),
        pltpu.VMEM((frames * points, 4 * chan), BF16),
        pltpu.VMEM((4, rows // 2, frames, half, width), F32),
    ]
    outs = call(
        functools.partial(encode_body, links=links, rows=rows, strip=strip),
        shapes,
        args,
        scratch=scratch,
        room=32,
        manual=(1, 2, 3, 4, 5, *range(6 + links, 10 + links)),
    )
    return outs[:4], outs[4:]


def gradients_body(*refs, links, scale_mid, scale_top):
    teachers, refs = refs[:links], refs[links:]
    spatial, mid, attended, student, keep, give, t_mid, t_top, g_mid, g_top = refs
    zhi, core = place()
    rows, padded, strip, chan = spatial.shape
    frames = padded - 2
    half_rows, _, half, width = t_top.shape
    base = rows * strip
    points = half_rows * half
    for k in range(links):
        origin = lax.rem(zhi - k + links, links)
        for s in range(2):
            t = 2 * origin + (core if s == 0 else 1 - core)
            t_mid[:, t] = teachers[k][s, :base].reshape(rows, strip, chan)
            low = teachers[k][s, base : base + points].astype(F32)
            high = teachers[k][s, base + points :].astype(F32)
            t_top[:, t, :, :chan] = low.reshape(half_rows, half, chan)
            t_top[:, t, :, chan:] = high.reshape(half_rows, half, chan)
    count = rows * frames * strip
    diff = (mid[...].astype(F32) - t_mid[...].reshape(count, chan).astype(F32)).astype(BF16)
    dims = (((0,), (0,)), ((), ()))
    for m in range(3):
        g_mid[m * chan : (m + 1) * chan] = (
            lax.dot_general(
                spatial[:, m : m + frames].reshape(count, chan),
                diff,
                dims,
                preferred_element_type=F32,
            )
            * scale_mid
        )
    diff = (
        student[...].astype(F32) - t_top[...].reshape(frames * points, width)
    ).astype(BF16)
    g_top[...] = lax.dot_general(attended[...], diff, dims, preferred_element_type=F32) * scale_top
    spaces = 2 * keep.shape[0]
    n_mid = g_mid.shape[0] // (frames * spaces)
    n_top = g_top.shape[0] // (frames * spaces)
    for c in range(2):

        @pl.when(core == c)
        def _():
            for side, ref in ((c, keep), (1 - c, give)):
                for z in range(links):
                    for p in range(spaces):
                        shard = (2 * z + side) * spaces + p
                        piece = ref.at[p // 2, z, p % 2]
                        rows_mid = g_mid[shard * n_mid : (shard + 1) * n_mid]
                        rows_top = g_top[shard * n_top : (shard + 1) * n_top]
                        row = 0
                        for block in (rows_mid, rows_top):
                            for h in range(block.shape[1] // LANES):
                                part = block[:, h * LANES : (h + 1) * LANES]
                                piece[row : row + block.shape[0]] = part.astype(ref.dtype)
                                row += block.shape[0]


def gradients(teachers, spatial, mid, attended, student, links, spaces, scale_mid, scale_top):
    rows, padded, strip, chan = spatial.shape
    frames = padded - 2
    width = attended.shape[-1]
    height = (3 * chan * chan + width * width) // (frames * spaces * LANES)
    return call(
        functools.partial(
            gradients_body, links=links, scale_mid=scale_mid, scale_top=scale_top
        ),
        [
            jax.ShapeDtypeStruct((spaces // 2, links, 2, height, LANES), F32),
            jax.ShapeDtypeStruct((spaces // 2, links, 2, height, LANES), BF16),
        ],
        (*teachers, spatial, mid, attended, student),
        scratch=[
            pltpu.VMEM((rows, frames, strip, chan), BF16),
            pltpu.VMEM((rows // 2, frames, strip // 2, width), F32),
            pltpu.VMEM((3 * chan, chan), F32),
            pltpu.VMEM((width, width), F32),
        ],
        room=16,
    )


def unpack_body(*refs, links):
    mine, swapped, out = refs[:links], refs[links], refs[links + 1]
    zhi, core = place()
    half_rows, cols, width = out.shape
    half = cols // (2 * links)
    for k in range(links):
        origin = lax.rem(zhi - k + links, links)
        own = mine[k][0].astype(F32).reshape(half_rows, half, width)
        other = swapped[k].astype(F32).reshape(half_rows, half, width)
        first = jnp.where(core == 0, own, other)
        second = jnp.where(core == 0, other, own)
        begin = pl.multiple_of(origin * 2 * half, 2 * half)
        out[:, pl.ds(begin, 2 * half), :] = jnp.concatenate([first, second], 1).astype(BF16)


def finish_body(*refs):
    parts, mid, top = refs[:-2], refs[-2], refs[-1]
    total = functools.reduce(jnp.add, [part[...] for part in parts])
    row = 0
    for out in (mid, top):
        count, cols = out.shape
        for h in range(cols // LANES):
            out[:, h * LANES : (h + 1) * LANES] = total[row : row + count]
            row += count


def local(
    feats, w_spatial, w_temporal, teacher_mid, w_down, w_query, w_key, w_value, w_out, teacher_top
):
    frames = lax.axis_size("tm")
    spaces = lax.axis_size("space")
    clips = lax.axis_size("dp")
    links = frames // 2
    devices_all = clips * frames * spaces
    own = feats[0, 0]
    rows, cols, chan = own.shape
    strip = cols // frames
    half_rows, half_cols, width = teacher_top.shape[2:]
    points = half_rows * (half_cols // frames)

    def swap(block):
        return lax.ppermute(block, "tm", [(i, i ^ 1) for i in range(frames)])

    def spread(pieces):
        return [pieces[0]] + [
            lax.ppermute(pieces[k], "tm", [(i, (i + 2 * k) % frames) for i in range(frames)])
            for k in range(1, links)
        ]

    columns = [list(range(c, frames, 2)) for c in range(2)]

    def gather(pieces):
        return lax.all_to_all(pieces, "tm", 0, 0, axis_index_groups=columns, tiled=True)

    ring = [(i, (i + 1) % spaces) for i in range(spaces)]
    above = lax.ppermute(own[rows - 1], "space", ring)
    below = lax.ppermute(own[0], "space", [(j, i) for i, j in ring])
    cells = pack_main(own, swap(own), links)
    cells = spread(cells)
    other = (swap(above), swap(below))
    halo = pack_halo((above, below), other, links)
    halos = gather(halo)
    t_mid, t_top = teacher_mid[0, 0], teacher_top[0, 0]
    teachers = pack_teacher(t_mid, swap(t_mid), t_top, swap(t_top), links)
    teachers = spread(teachers)

    w_proj = (w_query, w_key, w_value, w_out)
    saved, pieces = encode(
        cells, halos, w_spatial, w_temporal, w_down, w_proj, links, rows, strip
    )
    returned = spread(pieces)
    swapped = swap(jnp.stack([piece[1] for piece in returned]))
    home = call(
        functools.partial(unpack_body, links=links),
        [jax.ShapeDtypeStruct((half_rows, half_cols, width), BF16)],
        (*returned, swapped),
    )[0]

    keep, give = gradients(
        teachers,
        *saved,
        links,
        spaces,
        1.0 / math.sqrt(rows * cols * devices_all),
        1.0 / math.sqrt(points * frames * devices_all),
    )
    part = (keep + swap(give).astype(F32)).astype(BF16)
    lines = [list(range(a, spaces, 2)) for a in range(2)]
    part = lax.all_to_all(part, "space", 0, 0, axis_index_groups=lines, tiled=True)
    part = jnp.sum(part.astype(F32), 0).astype(BF16)
    part = part.reshape(frames, *part.shape[2:])
    groups = [
        [(2 * z + c) * spaces + p + a for z in range(links) for a in range(2)]
        for c in range(2)
        for p in range(0, spaces, 2)
    ]
    part = lax.all_to_all(part, ("tm", "space"), 0, 0, axis_index_groups=groups, tiled=True)
    part = jnp.sum(part.astype(F32), 0)
    others = [lax.ppermute(part, "dp", [(i, i ^ k) for i in range(clips)]) for k in range(1, clips)]
    n_top = width // (frames * spaces)
    grad_temporal, grad_out = call(
        finish_body,
        [
            jax.ShapeDtypeStruct((3 * chan // (frames * spaces), chan), F32),
            jax.ShapeDtypeStruct((n_top, width), F32),
        ],
        (part, *others),
    )
    return (home[None, None], grad_temporal, grad_out)


def solution(mesh):
    return jax.shard_map(
        local,
        mesh=mesh,
        in_specs=(
            P("dp", "tm", "space", None, None),
            P(),
            P(),
            P("dp", "tm", "space", None, None),
            P(),
            P(),
            P(),
            P(),
            P(),
            P("dp", "tm", "space", None, None),
        ),
        out_specs=(
            P("dp", "tm", "space", None, None),
            P(("tm", "space"), None),
            P(("tm", "space"), None),
        ),
        check_vma=False,
    )
```
